32 devices in a mesh: dp: 16 (over z, x, core), seq: 2 (over y).
Axes of the slice: x: 2, y: 2, z: 4, core: 2. Of those that a mesh axis runs over, the one named last changes fastest.
Arguments:
- character_codes: int32 [16, 512, 50], P('dp', 'seq'), may hold values from 0 to 262
- word_lengths: int32 [16, 512], P('dp', 'seq'), may hold values from 1 to 50
- sequence_lengths: int32 [16], P('dp'), may hold values from 128 to 512, as said below
- character_table: bfloat16 [263, 16], replicated, may hold values from -6 to 6
- conv_width1: bfloat16 [16, 32], replicated, may hold values from -1.5 to 1.5
- conv_width2: bfloat16 [32, 32], replicated, may hold values from -1 to 1
- conv_width3: bfloat16 [48, 64], replicated, may hold values from -0.875 to 0.875
- conv_width4: bfloat16 [64, 128], replicated, may hold values from -0.75 to 0.75
- conv_width5: bfloat16 [80, 256], replicated, may hold values from -0.625 to 0.625
- conv_width6: bfloat16 [96, 512], replicated, may hold values from -0.625 to 0.625
- conv_width7: bfloat16 [112, 1024], replicated, may hold values from -0.5 to 0.5
- conv_bias: bfloat16 [2048], replicated, may hold values from -2.5 to -0.5
- highway_weight: bfloat16 [2048, 4096], P('dp'), may hold values from -0.125 to 0.125
- highway_bias: bfloat16 [4096], replicated, may hold values from -5 to 5
- projection: bfloat16 [2048, 768], P('dp'), may hold values from -0.125 to 0.125
- position_table: bfloat16 [512, 768], replicated, may hold values from -6 to 6
- attention_in: bfloat16 [768, 2304], P('dp'), may hold values from -0.3125 to 0.3125
- attention_out: bfloat16 [768, 768], P('dp'), may hold values from -0.875 to 0.875
- norm1_gain: bfloat16 [768], replicated, may hold values from 0.5 to 1.5
- norm1_bias: bfloat16 [768], replicated, may hold values from -1.5 to 1.5
- hidden_in: bfloat16 [768, 3072], P('dp'), may hold values from -0.21875 to 0.21875
- hidden_out: bfloat16 [3072, 768], P('dp'), may hold values from -0.15625 to 0.15625
- norm2_gain: bfloat16 [768], replicated, may hold values from 0.5 to 1.5
- norm2_bias: bfloat16 [768], replicated, may hold values from -1.5 to 1.5
- cotangent: bfloat16 [16, 512, 768], P('dp', 'seq'), may hold values from -6 to 6
Outputs:
- layer_out: bfloat16 [16, 512, 768], P('dp', 'seq')
- character_table_gradient: float32 [263, 16], replicated
- conv_width1_gradient: float32 [16, 32], replicated
- conv_width2_gradient: float32 [32, 32], replicated
- conv_width3_gradient: float32 [48, 64], replicated
- conv_width4_gradient: float32 [64, 128], replicated
- conv_width5_gradient: float32 [80, 256], replicated
- conv_width6_gradient: float32 [96, 512], replicated
- conv_width7_gradient: float32 [112, 1024], replicated
- conv_bias_gradient: float32 [2048], replicated
- highway_weight_gradient: float32 [2048, 4096], P('dp')
- highway_bias_gradient: float32 [4096], replicated
- projection_gradient: float32 [2048, 768], P('dp')
- position_table_gradient: float32 [512, 768], replicated
- attention_in_gradient: float32 [768, 2304], P('dp')
- attention_out_gradient: float32 [768, 768], P('dp')
- norm1_gain_gradient: float32 [768], replicated
- norm1_bias_gradient: float32 [768], replicated
- hidden_in_gradient: float32 [768, 3072], P('dp')
- hidden_out_gradient: float32 [3072, 768], P('dp')
- norm2_gain_gradient: float32 [768], replicated
- norm2_bias_gradient: float32 [768], replicated
The draws below stay inside these ranges and needn't reach their ends.
Inputs may be any that keep to these rules, and one draw needn't show every extreme that they name: `sequence_lengths`: keys at or after a sequence's length take no part in attention; the first sequence has all 512 words.
All inputs are finite; a program needn't handle non-finite values.
Results may differ from the reference program's by a relative error of at most 0.028.
The reference program's roundings to bfloat16 on the way count: a program that leaves them out, or rounds other values in their place, can miss the bound.
Values may be sent and summed in bfloat16 or wider, within the bound.
No kernel may reach another device: no remote copies, remote signals or barrier semaphores. Data moves between devices by JAX's collectives and lax.ppermute only.
A program may use at most 256 MiB of HBM per device.

```python
from functools import partial
import jax
import jax.numpy as jnp
from jax import lax

VOCAB = 263
CHAR_DIM = 16
CHARS = 50
FILTERS_W1 = 32
FILTERS_W2 = 32
FILTERS_W3 = 64
FILTERS_W4 = 128
FILTERS_W5 = 256
FILTERS_W6 = 512
FILTERS_W7 = 1024
FILTERS = 2048
D = 768
HEAD_DIM = 64
FF = 3072
LENGTH = 512
BATCH = 16


def draw_sequence_lengths(key, part):
    drawn = jax.random.randint(key, (BATCH,), LENGTH // 4, LENGTH + 1)
    return jnp.where(jnp.arange(BATCH) == 0, LENGTH, drawn).astype(jnp.int32)


def with_ends(values, rng, least, top_value):
    longest = values.shape.index(max(values.shape))
    spots = []
    for shift in (0, 1):
        where = [jax.random.randint(jax.random.fold_in(rng, axis), (), 0, length) for axis, length in enumerate(values.shape)]
        where[longest] = (where[longest] + shift) % values.shape[longest]
        spots.append(tuple(where))
    return values.at[spots[0]].set(least).at[spots[1]].set(top_value)


def levels(rng, dims, pieces, least, top_value):
    level, own = 1.0, jax.random.fold_in(rng, 6)
    for axis_at, parts in pieces:
        heights = jnp.exp(jax.random.uniform(jax.random.fold_in(own, axis_at), (parts,), jnp.float32, least / len(pieces), top_value / len(pieces)))
        level = level * jnp.repeat(heights, dims[axis_at] // parts).reshape([-1 if axis == axis_at else 1 for axis in range(len(dims))])
    return level


def scatter_about(own_key, shape, scale, most, shards=(), kind=jnp.bfloat16):
    level = levels(own_key, shape, shards, -0.22, 0.18) if shards else 1.0
    result = jax.random.normal(own_key, shape, jnp.float32) * scale * level
    return jnp.minimum(jnp.maximum(result, -most), most).astype(kind)


def setup_inputs(seed: int = 0) -> dict:
    seeds = jax.random.split(jax.random.key(seed), 26)
    character_codes = with_ends(jax.random.randint(seeds[0], (BATCH, LENGTH, CHARS), 0, VOCAB), jax.random.fold_in(seeds[0], 1), 0, VOCAB - 1).astype(jnp.int32)
    word_lengths = with_ends(jax.random.randint(seeds[1], (BATCH, LENGTH), 1, CHARS + 1), jax.random.fold_in(seeds[1], 1), 1, CHARS).astype(jnp.int32)
    sequence_lengths = draw_sequence_lengths(jax.random.fold_in(seeds[25], 71), 0)
    character_table = scatter_about(seeds[3], (VOCAB, CHAR_DIM), 1.0, 6.0)
    conv_width1 = scatter_about(seeds[4], (CHAR_DIM, FILTERS_W1), CHAR_DIM ** -0.5, 1.5)
    conv_width2 = scatter_about(seeds[5], (2 * CHAR_DIM, FILTERS_W2), (2 * CHAR_DIM) ** -0.5, 1.0)
    conv_width3 = scatter_about(seeds[6], (3 * CHAR_DIM, FILTERS_W3), (3 * CHAR_DIM) ** -0.5, 0.875)
    conv_width4 = scatter_about(seeds[7], (4 * CHAR_DIM, FILTERS_W4), (4 * CHAR_DIM) ** -0.5, 0.75)
    conv_width5 = scatter_about(seeds[8], (5 * CHAR_DIM, FILTERS_W5), (5 * CHAR_DIM) ** -0.5, 0.625)
    conv_width6 = scatter_about(seeds[9], (6 * CHAR_DIM, FILTERS_W6), (6 * CHAR_DIM) ** -0.5, 0.625)
    conv_width7 = scatter_about(seeds[10], (7 * CHAR_DIM, FILTERS_W7), (7 * CHAR_DIM) ** -0.5, 0.5)
    conv_bias = jnp.clip(jax.random.uniform(seeds[11], (FILTERS,), jnp.float32, -2.5, -0.5), -2.5, -0.5).astype(jnp.bfloat16)
    highway_weight = scatter_about(seeds[12], (FILTERS, 2 * FILTERS), FILTERS ** -0.5, 0.125, ((0, 16),))
    highway_bias = scatter_about(seeds[13], (2 * FILTERS,), 1.0, 5.0)
    projection = scatter_about(seeds[14], (FILTERS, D), FILTERS ** -0.5, 0.125, ((0, 16),))
    position_table = scatter_about(seeds[15], (LENGTH, D), 1.0, 6.0)
    attention_in = scatter_about(seeds[16], (D, 3 * D), (D // 2) ** -0.5, 0.3125, ((0, 16),))
    attention_out = scatter_about(seeds[17], (D, D), (D // 16) ** -0.5, 0.875, ((0, 16),))
    norm1_gain = jnp.clip(1.0 + 0.1 * jax.random.normal(seeds[18], (D,), jnp.float32), 0.5, 1.5).astype(jnp.bfloat16)
    norm1_bias = scatter_about(seeds[19], (D,), 0.3, 1.5)
    hidden_in = scatter_about(seeds[20], (D, FF), D ** -0.5, 0.21875, ((0, 16),))
    hidden_out = scatter_about(seeds[21], (FF, D), (FF // 2) ** -0.5, 0.15625, ((0, 16),))
    norm2_gain = jnp.clip(1.0 + 0.1 * jax.random.normal(seeds[22], (D,), jnp.float32), 0.5, 1.5).astype(jnp.bfloat16)
    norm2_bias = scatter_about(seeds[23], (D,), 0.3, 1.5)
    cotangent = scatter_about(seeds[24], (BATCH, LENGTH, D), 1.0, 6.0, ((0, 16), (1, 2)))
    return {"character_codes": character_codes, "word_lengths": word_lengths, "sequence_lengths": sequence_lengths, "character_table": character_table, "conv_width1": conv_width1, "conv_width2": conv_width2, "conv_width3": conv_width3, "conv_width4": conv_width4, "conv_width5": conv_width5, "conv_width6": conv_width6, "conv_width7": conv_width7, "conv_bias": conv_bias, "highway_weight": highway_weight, "highway_bias": highway_bias, "projection": projection, "position_table": position_table, "attention_in": attention_in, "attention_out": attention_out, "norm1_gain": norm1_gain, "norm1_bias": norm1_bias, "hidden_in": hidden_in, "hidden_out": hidden_out, "norm2_gain": norm2_gain, "norm2_bias": norm2_bias, "cotangent": cotangent}


@jax.custom_vjp
def low(v):
    return lax.optimization_barrier(v.astype(jnp.bfloat16)).astype(jnp.float32)

@jax.custom_vjp
def low_back(v):
    return v

def low_keep(v):
    return (low(v), None)

def low_pass(kept, grad):
    return (grad,)

def back_keep(v):
    return (v, None)

def back_low(kept, grad):
    return (low(grad),)
low.defvjp(low_keep, low_pass)
low_back.defvjp(back_keep, back_low)
exact_mode = lax.Precision.HIGHEST
exact_gelu = partial(jax.nn.gelu, approximate=False)

def product(left, right):
    return jnp.dot(left, right, precision=exact_mode, preferred_element_type=jnp.float32)

def layer_norm(value, gain, bias):
    mean = lax.optimization_barrier(jnp.mean(value, axis=-1, keepdims=True))
    centered = value - mean
    spread = lax.optimization_barrier(jnp.mean(centered * centered, axis=-1, keepdims=True))
    return centered * lax.rsqrt(spread + 1e-12) * gain + bias

def highway_mix(gates, hidden):
    filters = hidden.shape[1]
    carry = jax.nn.sigmoid(gates[:, filters:])
    return carry * hidden + (1.0 - carry) * jax.nn.relu(gates[:, :filters])

def character_layer(codes, lengths, table, kernels, conv_bias):
    embed = low_back(jnp.take(table, codes, axis=0))
    letters = codes.shape[1]
    features = table.shape[1]
    pooled = []
    for kernel in kernels:
        width = kernel.shape[0] // features
        count = letters - width + 1
        window = jnp.concatenate([embed[:, shift:shift + count] for shift in range(width)], axis=2)
        conv = low_back(jnp.einsum('wpk,kc->wpc', window, kernel, precision=exact_mode))
        limit = jnp.maximum(lengths - width + 1, 1)
        valid = jnp.arange(count, dtype=jnp.int32)[None, :] < limit[:, None]
        pooled.append(lax.optimization_barrier(jnp.max(jnp.where(valid[:, :, None], conv, -1e+30), axis=1)))
    return jax.nn.relu(jnp.concatenate(pooled, axis=1) + conv_bias)

def forward(weights, codes, lengths, sequence_length):
    table = weights[0]
    kernels = weights[1:8]
    conv_bias, highway_weight, highway_bias, projection, position_table, attention_in, attention_out, norm1_gain, norm1_bias, hidden_in, hidden_out, norm2_gain, norm2_bias = weights[8:]
    hidden0 = character_layer(codes, lengths, table, kernels, conv_bias)
    gates = low_back(product(low(hidden0), highway_weight) + highway_bias)
    hidden1 = highway_mix(gates, hidden0)
    embedded = low_back(product(low(hidden1), projection)) + position_table
    length = embedded.shape[0]
    model = embedded.shape[1]
    heads = model // HEAD_DIM
    projected = low(low_back(product(low(embedded), attention_in)))
    query = projected[:, :model].reshape(length, heads, HEAD_DIM)
    keys = projected[:, model:2 * model].reshape(length, heads, HEAD_DIM)
    values = projected[:, 2 * model:].reshape(length, heads, HEAD_DIM)
    keep = jnp.arange(length, dtype=jnp.int32) < sequence_length
    raw = jnp.einsum('qhd,khd->hqk', query, keys, precision=exact_mode) * 0.125
    scores = low_back(jnp.where(keep[None, None, :], raw, -1e+30))
    probs = jax.nn.softmax(scores, axis=-1)
    attended = jnp.einsum('hqk,khd->qhd', low(probs), values, precision=exact_mode).reshape(length, model)
    attended = low(low_back(attended))
    joined = embedded + low_back(product(attended, attention_out))
    normed1 = layer_norm(joined, norm1_gain, norm1_bias)
    inner = low_back(product(low(normed1), hidden_in))
    outer = low_back(product(low(exact_gelu(inner)), hidden_out))
    return layer_norm(normed1 + outer, norm2_gain, norm2_bias)

def reference(character_codes, word_lengths, sequence_lengths, character_table, conv_width1, conv_width2, conv_width3, conv_width4, conv_width5, conv_width6, conv_width7, conv_bias, highway_weight, highway_bias, projection, position_table, attention_in, attention_out, norm1_gain, norm1_bias, hidden_in, hidden_out, norm2_gain, norm2_bias, cotangent):
    weights = tuple((item.astype(jnp.float32) for item in (character_table, conv_width1, conv_width2, conv_width3, conv_width4, conv_width5, conv_width6, conv_width7, conv_bias, highway_weight, highway_bias, projection, position_table, attention_in, attention_out, norm1_gain, norm1_bias, hidden_in, hidden_out, norm2_gain, norm2_bias)))

    def per_sequence(totals, inputs):
        codes, lengths, sequence_length, seed_grad = inputs
        output, pullback = jax.vjp(lambda params: forward(params, codes, lengths, sequence_length), weights)
        grads = pullback(seed_grad.astype(jnp.float32))[0]
        return (jax.tree.map(jnp.add, totals, grads), output.astype(jnp.bfloat16))
    start = tuple((jnp.zeros(item.shape, jnp.float32) for item in weights))
    totals, outputs = lax.scan(per_sequence, start, (character_codes, word_lengths, sequence_lengths, cotangent))
    return (outputs, totals[0], totals[1], totals[2], totals[3], totals[4], totals[5], totals[6], totals[7], totals[8], totals[9], totals[10], totals[11], totals[12], totals[13], totals[14], totals[15], totals[16], totals[17], totals[18], totals[19], totals[20])
```

```python
from functools import partial
import math

import jax
import jax.numpy as jnp
from jax import lax
from jax.experimental import pallas as pl
from jax.experimental.pallas import tpu as pltpu
from jax.sharding import PartitionSpec as P

HEAD_DIM = 64


exact_gelu = partial(jax.nn.gelu, approximate=False)


def layer_norm(value, gain, bias):
    mean = jnp.mean(value, axis=-1, keepdims=True)
    centered = value - mean
    spread = jnp.mean(centered * centered, axis=-1, keepdims=True)
    return centered * lax.rsqrt(spread + 1e-12) * gain + bias


def highway_mix(gates, hidden):
    filters = hidden.shape[1]
    carry = jax.nn.sigmoid(gates[:, filters:])
    return carry * hidden + (1.0 - carry) * jax.nn.relu(gates[:, :filters])


WIDTHS = 7
LANES = 128
NEG = -1e30


def conv_forward_kernel(spread_ref, lens_ref, weight_ref, pooled_ref, ties_ref, window_ref, flipped_ref, scores_ref):
    letters, words, _ = spread_ref.shape
    channels = weight_ref.shape[1]
    lane = lax.broadcasted_iota(jnp.int32, (words, LANES), 1)
    slot = lane // 16
    limit = jnp.maximum(lens_ref[...] - (lane - 16 * WIDTHS), 1)
    for p in range(letters):
        window = jnp.zeros((words, LANES), jnp.float32)
        for j in range(WIDTHS):
            if p + j < letters:
                window = jnp.where(slot == j, spread_ref[p + j].astype(jnp.float32), window)
        flag = jnp.where((lane >= 16 * WIDTHS) & (lane < 17 * WIDTHS) & (p >= limit), 1.0, window)
        window_ref[p * words:(p + 1) * words] = flag.astype(jnp.bfloat16)
    flipped_ref[...] = window_ref[...].T
    tile = 256
    for c in range(0, channels, tile):
        scores_ref[...] = jnp.dot(window_ref[...], weight_ref[:, c:c + tile], preferred_element_type=jnp.float32)
        for r in range(0, words, 16):
            top = scores_ref[r:r + 16]
            for p in range(1, letters):
                top = jnp.maximum(top, scores_ref[p * words + r:p * words + r + 16])
            count = jnp.zeros((16, tile), jnp.float32)
            for p in range(letters):
                count += jnp.where(scores_ref[p * words + r:p * words + r + 16] == top, 1.0, 0.0)
            pooled_ref[r:r + 16, c:c + tile] = top
            ties_ref[r:r + 16, c:c + tile] = count


def conv_backward_kernel(window_ref, flipped_ref, codes_ref, weight_ref, turned_ref, pooled_ref, share_in_ref,
                         grad_ref, table_ref, share_ref, scores_ref, spread_ref, letters):
    rows = window_ref.shape[0]
    words = rows // letters
    channels = weight_ref.shape[1]
    vocab = table_ref.shape[0]
    tile = 256

    @pl.when(pl.program_id(0) == 0)
    def _():
        grad_ref[...] = jnp.zeros_like(grad_ref)
        table_ref[...] = jnp.zeros_like(table_ref)

    for c in range(0, channels, tile):
        scores_ref[...] = jnp.dot(window_ref[...], weight_ref[:, c:c + tile], preferred_element_type=jnp.float32)
        for r in range(0, words, 16):
            top = pooled_ref[r:r + 16, c:c + tile]
            part = share_in_ref[r:r + 16, c:c + tile]
            for p in range(letters):
                hit = scores_ref[p * words + r:p * words + r + 16] == top
                share_ref[p * words + r:p * words + r + 16, c:c + tile] = jnp.where(hit, part, 0.0).astype(jnp.bfloat16)
    grad_ref[...] += jnp.dot(flipped_ref[...], share_ref[...], preferred_element_type=jnp.float32)
    scores_ref[:, :LANES] = jnp.dot(share_ref[...], turned_ref[...], preferred_element_type=jnp.float32)
    slot = lax.broadcasted_iota(jnp.int32, (words, LANES), 1) // 16
    for c in range(letters):
        spread = jnp.zeros((words, LANES), jnp.float32)
        for j in range(WIDTHS):
            if c - j >= 0:
                spread = jnp.where(slot == j, scores_ref[(c - j) * words:(c - j + 1) * words, :LANES], spread)
        spread_ref[c * words:(c + 1) * words] = spread.astype(jnp.bfloat16)
    onehot = jnp.where(lax.broadcasted_iota(jnp.int32, (vocab, rows), 0) == codes_ref[0], 1.0, 0.0).astype(jnp.bfloat16)
    table_ref[...] += jnp.dot(onehot, spread_ref[...], preferred_element_type=jnp.float32)


def conv_forward(spread, lens, weight, block):
    letters, words, _ = spread.shape
    channels = weight.shape[1]
    steps = words // block
    rows = letters * block
    f32 = jnp.float32
    return pl.pallas_call(
        conv_forward_kernel,
        grid=(steps,),
        in_specs=[
            pl.BlockSpec((letters, block, LANES), lambda i: (0, i, 0)),
            pl.BlockSpec((block, 1), lambda i: (i, 0)),
            pl.BlockSpec((LANES, channels), lambda i: (0, 0)),
        ],
        out_specs=[
            pl.BlockSpec((block, channels), lambda i: (i, 0)),
            pl.BlockSpec((block, channels), lambda i: (i, 0)),
            pl.BlockSpec((rows, LANES), lambda i: (i, 0)),
            pl.BlockSpec((LANES, rows), lambda i: (0, i)),
        ],
        out_shape=[
            jax.ShapeDtypeStruct((words, channels), f32),
            jax.ShapeDtypeStruct((words, channels), f32),
            jax.ShapeDtypeStruct((steps * rows, LANES), jnp.bfloat16),
            jax.ShapeDtypeStruct((LANES, steps * rows), jnp.bfloat16),
        ],
        scratch_shapes=[pltpu.VMEM((rows, 256), f32)],
        compiler_params=pltpu.CompilerParams(dimension_semantics=("arbitrary",)),
        name="conv_forward",
    )(spread, lens, weight)


def conv_backward(window, flipped, codes, weight, turned, pooled, share, vocab, block):
    words, channels = pooled.shape
    steps = words // block
    rows = window.shape[0] // steps
    letters = rows // block
    f32 = jnp.float32
    vocab = -(-vocab // 16) * 16

    def kernel(*refs):
        conv_backward_kernel(*refs, letters=letters)

    return pl.pallas_call(
        kernel,
        grid=(steps,),
        in_specs=[
            pl.BlockSpec((rows, LANES), lambda i: (i, 0)),
            pl.BlockSpec((LANES, rows), lambda i: (0, i)),
            pl.BlockSpec((1, 1, rows), lambda i: (i, 0, 0)),
            pl.BlockSpec((LANES, channels), lambda i: (0, 0)),
            pl.BlockSpec((channels, LANES), lambda i: (0, 0)),
            pl.BlockSpec((block, channels), lambda i: (i, 0)),
            pl.BlockSpec((block, channels), lambda i: (i, 0)),
        ],
        out_specs=[
            pl.BlockSpec((LANES, channels), lambda i: (0, 0)),
            pl.BlockSpec((vocab, LANES), lambda i: (0, 0)),
        ],
        out_shape=[
            jax.ShapeDtypeStruct((LANES, channels), f32),
            jax.ShapeDtypeStruct((vocab, LANES), f32),
        ],
        scratch_shapes=[
            pltpu.VMEM((rows, channels), jnp.bfloat16),
            pltpu.VMEM((rows, 256), f32),
            pltpu.VMEM((rows, LANES), jnp.bfloat16),
        ],
        compiler_params=pltpu.CompilerParams(dimension_semantics=("arbitrary",)),
        name="conv_backward",
    )(window, flipped, codes, weight, turned, pooled, share)


def merged_weight(kernels, features):
    columns = []
    for kernel in kernels:
        width = kernel.shape[0] // features
        channels = kernel.shape[1]
        marks = jnp.zeros((LANES - WIDTHS * features, channels), kernel.dtype).at[width - 1].set(NEG)
        columns.append(jnp.concatenate([kernel, jnp.zeros(((WIDTHS - width) * features, channels), kernel.dtype), marks], axis=0))
    return jnp.concatenate(columns, axis=1)


def spread_letters(codes, table):
    vocab, features = table.shape
    words, letters = codes.shape
    wide = jnp.tile(table, (1, LANES // features))
    onehot = (codes.T.reshape(-1, 1) == jnp.arange(vocab, dtype=jnp.int32)[None, :]).astype(jnp.bfloat16)
    return jnp.dot(onehot, wide, preferred_element_type=jnp.float32).astype(jnp.bfloat16).reshape(letters, words, LANES)


def score_heads(query_heads, key_heads, keep):
    raw = (
        jnp.einsum("qhd,khd->hqk", query_heads, key_heads, preferred_element_type=jnp.float32)
        * 0.125
    )
    return jnp.where(keep[None, None, :], raw, -1e30)


def body(
    character_codes,
    word_lengths,
    sequence_lengths,
    character_table,
    conv_width1,
    conv_width2,
    conv_width3,
    conv_width4,
    conv_width5,
    conv_width6,
    conv_width7,
    conv_bias,
    highway_weight,
    highway_bias,
    projection,
    position_table,
    attention_in,
    attention_out,
    norm1_gain,
    norm1_bias,
    hidden_in,
    hidden_out,
    norm2_gain,
    norm2_bias,
    cotangent,
):
    kernels = (
        conv_width1,
        conv_width2,
        conv_width3,
        conv_width4,
        conv_width5,
        conv_width6,
        conv_width7,
    )
    highway_full, projection_full = (
        lax.all_gather(highway_weight, "dp", axis=0, tiled=True),
        lax.all_gather(projection, "dp", axis=0, tiled=True),
    )
    codes = character_codes[0]
    lengths = word_lengths[0]
    words = codes.shape[0]
    letters = codes.shape[1]
    block = math.gcd(words, 64)
    steps = words // block
    features = character_table.shape[1]
    conv_weight = merged_weight(kernels, features)
    pooled, ties, windows, flipped = conv_forward(
        spread_letters(codes, character_table), lengths[:, None], conv_weight, block
    )
    biased = pooled + conv_bias.astype(jnp.float32)
    hidden0 = jax.nn.relu(biased)
    hidden0_low = hidden0.astype(jnp.bfloat16)
    attention_full, output_full, inward_full, outward_full = (
        lax.all_gather(attention_in, "dp", axis=0, tiled=True),
        lax.all_gather(attention_out, "dp", axis=0, tiled=True),
        lax.all_gather(hidden_in, "dp", axis=0, tiled=True),
        lax.all_gather(hidden_out, "dp", axis=0, tiled=True),
    )
    gates = jnp.dot(
        hidden0_low, highway_full, preferred_element_type=jnp.float32
    ) + highway_bias.astype(jnp.float32)
    hidden1 = highway_mix(gates, hidden0)
    hidden1_low = hidden1.astype(jnp.bfloat16)
    offset = lax.axis_index("seq") * words
    positions = lax.dynamic_slice_in_dim(position_table, offset, words, 0).astype(jnp.float32)
    embedded = jnp.dot(hidden1_low, projection_full, preferred_element_type=jnp.float32) + positions
    embedded_low = embedded.astype(jnp.bfloat16)
    model = embedded.shape[1]
    heads = model // HEAD_DIM
    projected = jnp.dot(embedded_low, attention_full, preferred_element_type=jnp.float32).astype(
        jnp.bfloat16
    )
    gathered = lax.all_gather(projected[:, model:], "seq", axis=0, tiled=True)
    length = gathered.shape[0]
    query_heads = projected[:, :model].reshape(words, heads, HEAD_DIM)
    key_heads = gathered[:, :model].reshape(length, heads, HEAD_DIM)
    value_heads = gathered[:, model:].reshape(length, heads, HEAD_DIM)
    keep = jnp.arange(length, dtype=jnp.int32) < sequence_lengths[0]
    scores = score_heads(query_heads, key_heads, keep)
    top = jnp.max(scores, axis=-1, keepdims=True)
    unnormalized = jnp.exp(scores - top)
    total = jnp.sum(unnormalized, axis=-1, keepdims=True)
    probs_low = (unnormalized / total).astype(jnp.bfloat16)
    attended = jnp.einsum(
        "hqk,khd->qhd", probs_low, value_heads, preferred_element_type=jnp.float32
    )
    attended = attended.reshape(words, model).astype(jnp.bfloat16)
    joined = embedded + jnp.dot(attended, output_full, preferred_element_type=jnp.float32)
    gain1 = norm1_gain.astype(jnp.float32)
    shift1 = norm1_bias.astype(jnp.float32)
    gain2 = norm2_gain.astype(jnp.float32)
    shift2 = norm2_bias.astype(jnp.float32)
    normed1 = layer_norm(joined, gain1, shift1)
    normed1_low = normed1.astype(jnp.bfloat16)
    inner = jnp.dot(normed1_low, inward_full, preferred_element_type=jnp.float32)
    active = exact_gelu(inner).astype(jnp.bfloat16)
    summed = normed1 + jnp.dot(active, outward_full, preferred_element_type=jnp.float32)
    layer_out = layer_norm(summed, gain2, shift2).astype(jnp.bfloat16)
    seed_grad = cotangent[0].astype(jnp.float32)
    _, norm2_pull = jax.vjp(layer_norm, summed, gain2, shift2)
    grad_summed, norm2_gain_grad, norm2_bias_grad = norm2_pull(seed_grad)
    grad_outer = grad_summed.astype(jnp.bfloat16)
    hidden_out_grad = jnp.einsum(
        "tf,td->fd", active, grad_outer, preferred_element_type=jnp.float32
    )
    grad_active = jnp.einsum(
        "td,fd->tf", grad_outer, outward_full, preferred_element_type=jnp.float32
    )
    _, gelu_pull = jax.vjp(exact_gelu, inner)
    grad_inner = gelu_pull(grad_active)[0].astype(jnp.bfloat16)
    hidden_in_grad = jnp.einsum(
        "td,tf->df", normed1_low, grad_inner, preferred_element_type=jnp.float32
    )
    grad_normed1 = grad_summed + jnp.einsum(
        "tf,df->td", grad_inner, inward_full, preferred_element_type=jnp.float32
    )
    _, norm1_pull = jax.vjp(layer_norm, joined, gain1, shift1)
    grad_joined, norm1_gain_grad, norm1_bias_grad = norm1_pull(grad_normed1)
    grad_branch = grad_joined.astype(jnp.bfloat16)
    attention_out_grad = jnp.einsum(
        "td,te->de", attended, grad_branch, preferred_element_type=jnp.float32
    )
    grad_attended = jnp.einsum(
        "te,de->td", grad_branch, output_full, preferred_element_type=jnp.float32
    ).astype(jnp.bfloat16)
    grad_heads = grad_attended.reshape(words, heads, HEAD_DIM)
    probs = jnp.exp(score_heads(query_heads, key_heads, keep) - top) / total
    probs_again = probs.astype(jnp.bfloat16)
    grad_probs = jnp.einsum(
        "qhd,khd->hqk", grad_heads, value_heads, preferred_element_type=jnp.float32
    )
    grad_scores = (
        probs * (grad_probs - jnp.sum(probs * grad_probs, axis=-1, keepdims=True))
    ).astype(jnp.bfloat16)
    grad_query = (
        jnp.einsum("hqk,khd->qhd", grad_scores, key_heads, preferred_element_type=jnp.float32)
        * 0.125
    )
    count = lax.axis_size("seq") * words
    score_part = lax.slice_in_dim(grad_scores, 0, count, axis=2)
    prob_part = lax.slice_in_dim(probs_again, 0, count, axis=2)
    key_grad = (
        jnp.einsum("hqk,qhd->khd", score_part, query_heads, preferred_element_type=jnp.float32)
        * 0.125
    )
    value_grad = jnp.einsum(
        "hqk,qhd->khd", prob_part, grad_heads, preferred_element_type=jnp.float32
    )
    grad_pairs = lax.psum_scatter(
        jnp.concatenate(
            [key_grad.reshape(count, model), value_grad.reshape(count, model)], axis=1
        ).astype(jnp.bfloat16),
        "seq",
        scatter_dimension=0,
        tiled=True,
    ).astype(jnp.float32)
    grad_projected = jnp.concatenate([grad_query.reshape(words, model), grad_pairs], axis=1).astype(
        jnp.bfloat16
    )
    attention_in_grad = jnp.einsum(
        "td,te->de", embedded_low, grad_projected, preferred_element_type=jnp.float32
    )
    grad_embedded = grad_joined + jnp.einsum(
        "te,de->td", grad_projected, attention_full, preferred_element_type=jnp.float32
    )
    position_grad = lax.dynamic_update_slice_in_dim(
        jnp.zeros((length, model), jnp.float32), grad_embedded, offset, 0
    )
    grad_mapped = grad_embedded.astype(jnp.bfloat16)
    projection_grad = jnp.einsum(
        "tf,td->fd", hidden1_low, grad_mapped, preferred_element_type=jnp.float32
    )
    grad_hidden1 = jnp.einsum(
        "td,fd->tf", grad_mapped, projection_full, preferred_element_type=jnp.float32
    )
    _, highway_pull = jax.vjp(highway_mix, gates, hidden0)
    grad_gates, grad_carry = highway_pull(grad_hidden1)
    grad_gates = grad_gates.astype(jnp.bfloat16)
    highway_grad = jnp.einsum(
        "tf,tg->fg", hidden0_low, grad_gates, preferred_element_type=jnp.float32
    )
    highway_bias_grad = jnp.sum(grad_gates.astype(jnp.float32), axis=0)
    grad_hidden0 = grad_carry + jnp.einsum(
        "tg,fg->tf", grad_gates, highway_full, preferred_element_type=jnp.float32
    )
    grad_pooled = jnp.where(biased > 0, grad_hidden0, 0.0)
    conv_bias_grad = jnp.sum(grad_pooled, axis=0)
    code_rows = codes.reshape(steps, block, letters).transpose(0, 2, 1)
    merged_grad, table_wide = conv_backward(
        windows,
        flipped,
        code_rows.reshape(steps, 1, letters * block),
        conv_weight,
        conv_weight.T,
        pooled,
        grad_pooled / ties,
        character_table.shape[0],
        block,
    )
    table_grad = sum(
        table_wide[: character_table.shape[0], shift * features : (shift + 1) * features]
        for shift in range(WIDTHS)
    )
    kernel_grads = []
    first = 0
    for kernel in kernels:
        kernel_grads.append(merged_grad[: kernel.shape[0], first : first + kernel.shape[1]])
        first = first + kernel.shape[1]
    share_highway, share_projection, share_attention, share_output, share_inward, share_outward = (
        lax.psum_scatter(highway_grad.astype(jnp.bfloat16), "dp", scatter_dimension=0, tiled=True),
        lax.psum_scatter(projection_grad.astype(jnp.bfloat16), "dp", scatter_dimension=0, tiled=True),
        lax.psum_scatter(attention_in_grad.astype(jnp.bfloat16), "dp", scatter_dimension=0, tiled=True),
        lax.psum_scatter(attention_out_grad.astype(jnp.bfloat16), "dp", scatter_dimension=0, tiled=True),
        lax.psum_scatter(hidden_in_grad.astype(jnp.bfloat16), "dp", scatter_dimension=0, tiled=True),
        lax.psum_scatter(hidden_out_grad.astype(jnp.bfloat16), "dp", scatter_dimension=0, tiled=True),
    )
    highway_total, projection_total, attention_total, output_total, inward_total, outward_total = (
        lax.psum(share_highway.astype(jnp.bfloat16), "seq").astype(jnp.float32),
        lax.psum(share_projection.astype(jnp.bfloat16), "seq").astype(jnp.float32),
        lax.psum(share_attention.astype(jnp.bfloat16), "seq").astype(jnp.float32),
        lax.psum(share_output.astype(jnp.bfloat16), "seq").astype(jnp.float32),
        lax.psum(share_inward.astype(jnp.bfloat16), "seq").astype(jnp.float32),
        lax.psum(share_outward.astype(jnp.bfloat16), "seq").astype(jnp.float32),
    )
    small = lax.psum(
        (
            table_grad,
            kernel_grads[0],
            kernel_grads[1],
            kernel_grads[2],
            kernel_grads[3],
            kernel_grads[4],
            kernel_grads[5],
            kernel_grads[6],
            conv_bias_grad,
            highway_bias_grad,
            position_grad,
            norm1_gain_grad,
            norm1_bias_grad,
            norm2_gain_grad,
            norm2_bias_grad,
        ),
        ("dp", "seq"),
    )
    return (
        layer_out[None],
        small[0],
        small[1],
        small[2],
        small[3],
        small[4],
        small[5],
        small[6],
        small[7],
        small[8],
        highway_total,
        small[9],
        projection_total,
        small[10],
        attention_total,
        output_total,
        small[11],
        small[12],
        inward_total,
        outward_total,
        small[13],
        small[14],
    )


def solution(mesh):
    placed = (
        P("dp", "seq", None),
        P("dp", "seq"),
        P("dp"),
        P(),
        P(),
        P(),
        P(),
        P(),
        P(),
        P(),
        P(),
        P(),
        P("dp", None),
        P(),
        P("dp", None),
        P(),
        P("dp", None),
        P("dp", None),
        P(),
        P(),
        P("dp", None),
        P("dp", None),
        P(),
        P(),
        P("dp", "seq", None),
    )
    return jax.shard_map(
        body,
        mesh=mesh,
        in_specs=placed,
        out_specs=(
            P("dp", "seq", None),
            P(),
            P(),
            P(),
            P(),
            P(),
            P(),
            P(),
            P(),
            P(),
            P("dp", None),
            P(),
            P("dp", None),
            P(),
            P("dp", None),
            P("dp", None),
            P(),
            P(),
            P("dp", None),
            P("dp", None),
            P(),
            P(),
        ),
        check_vma=False,
    )
```

```python
from functools import partial
import math

import jax
import jax.numpy as jnp
from jax import lax
from jax.experimental import pallas as pl
from jax.experimental.pallas import tpu as pltpu
from jax.sharding import PartitionSpec as P

HEAD_DIM = 64


exact_gelu = partial(jax.nn.gelu, approximate=False)


def layer_norm(value, gain, bias):
    mean = jnp.mean(value, axis=-1, keepdims=True)
    centered = value - mean
    spread = jnp.mean(centered * centered, axis=-1, keepdims=True)
    return centered * lax.rsqrt(spread + 1e-12) * gain + bias


def highway_mix(transform, gate, hidden):
    carry = jax.nn.sigmoid(gate)
    return carry * hidden + (1.0 - carry) * jax.nn.relu(transform)


def place():
    spot = lax.axis_index("dp")
    return (spot // 4, (spot // 2) % 2, spot % 2)


def core_swap(value):
    size = lax.axis_size("dp")
    return lax.ppermute(value, "dp", [(spot, spot ^ 1) for spot in range(size)])


def middle_swap(value):
    size = lax.axis_size("dp")
    return lax.ppermute(value, "dp", [(spot, spot ^ 2) for spot in range(size)])


def outer_shift(value, steps):
    size = lax.axis_size("dp")
    return lax.ppermute(value, "dp", [(spot, (spot - 4 * steps) % size) for spot in range(size)])


def seq_swap(value):
    return lax.ppermute(value, "seq", [(0, 1), (1, 0)])


def after(value, *others):
    return lax.optimization_barrier((value,) + others)[0]


def pick(value, index, axis):
    return lax.dynamic_index_in_dim(value, index, axis, keepdims=False)


def outer_pieces(shard):
    return [shard] + [outer_shift(shard, steps) for steps in range(1, lax.axis_size("dp") // 4)]


def gather_near(pieces):
    outer = place()[0]
    size = len(pieces)
    near = jnp.zeros((size,) + pieces[0].shape, pieces[0].dtype)
    for steps, piece in enumerate(pieces):
        near = lax.dynamic_update_index_in_dim(near, piece, (outer + steps) % size, 0)
    return near


def gather(values, side=None):
    _, middle, core = place()
    size = values[0].shape[0]
    shape = values[0].shape[1:]
    zeros = (0,) * len(shape)
    whole = jnp.zeros(((size, 2, 2) if side is None else (2, size, 2)) + shape, values[0].dtype)
    for flip, value in enumerate(values):
        flip_middle, flip_core = flip % 2, flip // 2
        if side is None:
            start = (0, middle ^ flip_middle, core ^ flip_core) + zeros
            value = value[:, None, None]
        else:
            start = (core ^ side ^ flip_core, 0, middle ^ flip_middle) + zeros
            value = value[None, :, None]
        whole = lax.dynamic_update_slice(whole, value, start)
    return whole


def scatter_core(parts, side=None):
    _, _, core = place()
    axis, slot = (2, core) if side is None else (0, core ^ side)
    other = core_swap(pick(parts, 1 - slot, axis).astype(jnp.bfloat16))
    return pick(parts, slot, axis).astype(jnp.float32) + other.astype(jnp.float32)


def scatter_middle(half):
    _, middle, _ = place()
    other = middle_swap(pick(half, 1 - middle, 1).astype(jnp.bfloat16))
    return pick(half, middle, 1) + other.astype(jnp.float32)


def scatter_outer(quarter):
    outer, _, _ = place()
    size = quarter.shape[0]
    rounded = quarter.astype(jnp.bfloat16)
    total = pick(quarter, outer, 0)
    for steps in range(1, size):
        sent = pick(rounded, (outer + size - steps) % size, 0)
        total = total + outer_shift(sent, steps).astype(jnp.float32)
    return total


def seq_sum(value):
    return value + seq_swap(value.astype(jnp.bfloat16)).astype(jnp.float32)


def own_blocks(value, axis):
    axis = axis % value.ndim
    size = lax.axis_size("dp")
    shape = value.shape
    split = shape[:axis] + (size // 2, 2, shape[axis] // size) + shape[axis + 1 :]
    chosen = pick(value.reshape(split), lax.axis_index("seq"), axis + 1)
    return chosen.reshape(shape[:axis] + (shape[axis] // 2,) + shape[axis + 1 :])


def interleave(own, other, piece):
    first = lax.axis_index("seq") == 0
    blocks = []
    for start in range(0, own.shape[1], piece):
        mine, theirs = own[:, start : start + piece], other[:, start : start + piece]
        blocks += [jnp.where(first, mine, theirs), jnp.where(first, theirs, mine)]
    return jnp.concatenate(blocks, axis=1)


def halves_of(value, piece):
    first = lax.axis_index("seq") == 0
    own, other = [], []
    for start in range(0, value.shape[1], 2 * piece):
        even, odd = value[:, start : start + piece], value[:, start + piece : start + 2 * piece]
        own.append(jnp.where(first, even, odd))
        other.append(jnp.where(first, odd, even))
    return jnp.concatenate(own, axis=1), jnp.concatenate(other, axis=1)


def by_seq(own, other):
    first = lax.axis_index("seq") == 0
    return jnp.stack([jnp.where(first, own, other), jnp.where(first, other, own)])


WIDTHS = 7
LANES = 128
NEG = -1e30


def conv_forward_kernel(spread_ref, lens_ref, weight_ref, pooled_ref, ties_ref, window_ref, flipped_ref, scores_ref):
    letters, words, _ = spread_ref.shape
    channels = weight_ref.shape[1]
    lane = lax.broadcasted_iota(jnp.int32, (words, LANES), 1)
    slot = lane // 16
    limit = jnp.maximum(lens_ref[...] - (lane - 16 * WIDTHS), 1)
    for p in range(letters):
        window = jnp.zeros((words, LANES), jnp.float32)
        for j in range(WIDTHS):
            if p + j < letters:
                window = jnp.where(slot == j, spread_ref[p + j].astype(jnp.float32), window)
        flag = jnp.where((lane >= 16 * WIDTHS) & (lane < 17 * WIDTHS) & (p >= limit), 1.0, window)
        window_ref[p * words:(p + 1) * words] = flag.astype(jnp.bfloat16)
    flipped_ref[...] = window_ref[...].T
    tile = 256

    def one_tile(index, _):
        c = pl.multiple_of(index * tile, tile)
        scores_ref[...] = jnp.dot(window_ref[...], weight_ref[:, pl.ds(c, tile)], preferred_element_type=jnp.float32)
        for r in range(0, words, 16):
            top = scores_ref[r:r + 16]
            for p in range(1, letters):
                top = jnp.maximum(top, scores_ref[p * words + r:p * words + r + 16])
            count = jnp.zeros((16, tile), jnp.float32)
            for p in range(letters):
                count += jnp.where(scores_ref[p * words + r:p * words + r + 16] == top, 1.0, 0.0)
            pooled_ref[r:r + 16, pl.ds(c, tile)] = top
            ties_ref[r:r + 16, pl.ds(c, tile)] = count
        return 0

    lax.fori_loop(0, channels // tile, one_tile, 0)


def conv_backward_kernel(window_ref, flipped_ref, codes_ref, weight_ref, turned_ref, pooled_ref, share_in_ref,
                         grad_ref, table_ref, share_ref, scores_ref, spread_ref, letters):
    rows = window_ref.shape[0]
    words = rows // letters
    channels = weight_ref.shape[1]
    vocab = table_ref.shape[0]
    tile = 256

    @pl.when(pl.program_id(0) == 0)
    def _():
        grad_ref[...] = jnp.zeros_like(grad_ref)
        table_ref[...] = jnp.zeros_like(table_ref)

    def one_tile(index, _):
        c = pl.multiple_of(index * tile, tile)
        scores_ref[...] = jnp.dot(window_ref[...], weight_ref[:, pl.ds(c, tile)], preferred_element_type=jnp.float32)
        for r in range(0, words, 16):
            top = pooled_ref[r:r + 16, pl.ds(c, tile)]
            part = share_in_ref[r:r + 16, pl.ds(c, tile)]
            for p in range(letters):
                hit = scores_ref[p * words + r:p * words + r + 16] == top
                share_ref[p * words + r:p * words + r + 16, pl.ds(c, tile)] = jnp.where(hit, part, 0.0).astype(jnp.bfloat16)
        return 0

    lax.fori_loop(0, channels // tile, one_tile, 0)
    grad_ref[...] += jnp.dot(flipped_ref[...], share_ref[...], preferred_element_type=jnp.float32)
    scores_ref[:, :LANES] = jnp.dot(share_ref[...], turned_ref[...], preferred_element_type=jnp.float32)
    slot = lax.broadcasted_iota(jnp.int32, (words, LANES), 1) // 16
    for c in range(letters):
        spread = jnp.zeros((words, LANES), jnp.float32)
        for j in range(WIDTHS):
            if c - j >= 0:
                spread = jnp.where(slot == j, scores_ref[(c - j) * words:(c - j + 1) * words, :LANES], spread)
        spread_ref[c * words:(c + 1) * words] = spread.astype(jnp.bfloat16)
    onehot = jnp.where(lax.broadcasted_iota(jnp.int32, (vocab, rows), 0) == codes_ref[0], 1.0, 0.0).astype(jnp.bfloat16)
    table_ref[...] += jnp.dot(onehot, spread_ref[...], preferred_element_type=jnp.float32)


def conv_forward(spread, lens, weight, block):
    letters, words, _ = spread.shape
    channels = weight.shape[1]
    steps = words // block
    rows = letters * block
    f32 = jnp.float32
    return pl.pallas_call(
        conv_forward_kernel,
        grid=(steps,),
        in_specs=[
            pl.BlockSpec((letters, block, LANES), lambda i: (0, i, 0)),
            pl.BlockSpec((block, 1), lambda i: (i, 0)),
            pl.BlockSpec((LANES, channels), lambda i: (0, 0)),
        ],
        out_specs=[
            pl.BlockSpec((block, channels), lambda i: (i, 0)),
            pl.BlockSpec((block, channels), lambda i: (i, 0)),
            pl.BlockSpec((rows, LANES), lambda i: (i, 0)),
            pl.BlockSpec((LANES, rows), lambda i: (0, i)),
        ],
        out_shape=[
            jax.ShapeDtypeStruct((words, channels), f32),
            jax.ShapeDtypeStruct((words, channels), f32),
            jax.ShapeDtypeStruct((steps * rows, LANES), jnp.bfloat16),
            jax.ShapeDtypeStruct((LANES, steps * rows), jnp.bfloat16),
        ],
        scratch_shapes=[pltpu.VMEM((rows, 256), f32)],
        compiler_params=pltpu.CompilerParams(dimension_semantics=("arbitrary",)),
        cost_estimate=pl.CostEstimate(
            flops=2 * LANES * steps * rows * channels,
            bytes_accessed=steps * rows * channels * 5,
            transcendentals=0,
        ),
        name="conv_forward",
    )(spread, lens, weight)


def conv_backward(window, flipped, codes, weight, turned, pooled, share, vocab, block, first, steps):
    words, channels = pooled.shape
    rows = window.shape[0] // (words // block)
    letters = rows // block
    f32 = jnp.float32
    vocab = -(-vocab // 16) * 16

    def kernel(*refs):
        conv_backward_kernel(*refs, letters=letters)

    return pl.pallas_call(
        kernel,
        grid=(steps,),
        in_specs=[
            pl.BlockSpec((rows, LANES), lambda i: (first + i, 0)),
            pl.BlockSpec((LANES, rows), lambda i: (0, first + i)),
            pl.BlockSpec((1, 1, rows), lambda i: (first + i, 0, 0)),
            pl.BlockSpec((LANES, channels), lambda i: (0, 0)),
            pl.BlockSpec((channels, LANES), lambda i: (0, 0)),
            pl.BlockSpec((block, channels), lambda i: (first + i, 0)),
            pl.BlockSpec((block, channels), lambda i: (first + i, 0)),
        ],
        out_specs=[
            pl.BlockSpec((LANES, channels), lambda i: (0, 0)),
            pl.BlockSpec((vocab, LANES), lambda i: (0, 0)),
        ],
        out_shape=[
            jax.ShapeDtypeStruct((LANES, channels), f32),
            jax.ShapeDtypeStruct((vocab, LANES), f32),
        ],
        scratch_shapes=[
            pltpu.VMEM((rows, channels), jnp.bfloat16),
            pltpu.VMEM((rows, 256), f32),
            pltpu.VMEM((rows, LANES), jnp.bfloat16),
        ],
        compiler_params=pltpu.CompilerParams(dimension_semantics=("arbitrary",)),
        cost_estimate=pl.CostEstimate(
            flops=6 * LANES * steps * rows * channels,
            bytes_accessed=steps * rows * channels * 8,
            transcendentals=0,
        ),
        name="conv_backward",
    )(window, flipped, codes, weight, turned, pooled, share)


def merge_kernel(*refs):
    whole_ref = refs[-1]
    whole_ref[...] = jnp.zeros_like(whole_ref)
    features = refs[0].shape[0]
    first = 0
    for width, kernel_ref in enumerate(refs[:-1], 1):
        channels = kernel_ref.shape[1]
        whole_ref[: width * features, first : first + channels] = kernel_ref[...]
        marks = lax.broadcasted_iota(jnp.int32, (16, channels), 0) == width - 1
        whole_ref[WIDTHS * features :, first : first + channels] = jnp.where(marks, NEG, 0.0).astype(jnp.bfloat16)
        first = first + channels


def merged_weight(kernels):
    channels = sum(kernel.shape[1] for kernel in kernels)
    return pl.pallas_call(
        merge_kernel, out_shape=jax.ShapeDtypeStruct((LANES, channels), jnp.bfloat16), name="merge_widths"
    )(*kernels)


def spread_letters(codes, table):
    vocab, features = table.shape
    words, letters = codes.shape
    wide = jnp.tile(table, (1, LANES // features))
    onehot = (codes.T.reshape(-1, 1) == jnp.arange(vocab, dtype=jnp.int32)[None, :]).astype(jnp.bfloat16)
    return jnp.dot(onehot, wide, preferred_element_type=jnp.float32).astype(jnp.bfloat16).reshape(letters, words, LANES)


def score_heads(query_heads, key_heads, keep):
    raw = (
        jnp.einsum("qhd,khd->hqk", query_heads, key_heads, preferred_element_type=jnp.float32)
        * 0.125
    )
    return jnp.where(keep[None, None, :], raw, -1e30)


def body(
    character_codes,
    word_lengths,
    sequence_lengths,
    character_table,
    conv_width1,
    conv_width2,
    conv_width3,
    conv_width4,
    conv_width5,
    conv_width6,
    conv_width7,
    conv_bias,
    highway_weight,
    highway_bias,
    projection,
    position_table,
    attention_in,
    attention_out,
    norm1_gain,
    norm1_bias,
    hidden_in,
    hidden_out,
    norm2_gain,
    norm2_bias,
    cotangent,
):
    kernels = (
        conv_width1,
        conv_width2,
        conv_width3,
        conv_width4,
        conv_width5,
        conv_width6,
        conv_width7,
    )
    f32 = jnp.float32
    low = jnp.bfloat16
    side = lax.axis_index("seq")
    outer, middle, core = place()
    size = lax.axis_size("dp")
    chips = size // 2
    words = character_codes.shape[1]
    letters = character_codes.shape[2]
    vocab, features = character_table.shape
    filters = conv_bias.shape[0]
    mine = filters // 2
    piece = filters // size
    half = piece // 2
    model = position_table.shape[1]
    block = math.gcd(words, 64)
    steps = words // block

    highway_shard = own_blocks(highway_weight.reshape(-1, 2, filters), 2)
    held = lax.dynamic_slice_in_dim(projection, core * half, half, 0)
    lent = lax.dynamic_slice_in_dim(projection, (1 - core) * half, half, 0)
    projection_shard = jnp.where(core == side, held, core_swap(lent))
    code_rows = jnp.concatenate([character_codes[0], word_lengths[0][:, None]], axis=1)
    code_rows = [code_rows, seq_swap(code_rows)]

    joint_shard = jnp.concatenate(
        [highway_shard.reshape(piece, filters), projection_shard.reshape(piece, model // 2)], axis=1
    )
    joint_all = lax.all_gather(joint_shard, "dp", axis=0, tiled=True)
    highway_parts = [joint_all[:, :mine], joint_all[:, mine:filters]]
    projection_full = joint_all[:, filters:].reshape(mine, model)
    attention_near = gather_near(outer_pieces(jnp.concatenate([attention_in, attention_out], axis=1)))
    attention_across = middle_swap(attention_near)
    attention_far = [core_swap(attention_near), core_swap(attention_across)]
    attention_all = gather((attention_near, attention_across, *attention_far)).reshape(model, -1)
    attention_full = attention_all[:, : 3 * model]
    output_full = attention_all[:, 3 * model :]

    def cut(grad, slots=False):
        lead = (2, size // 4, 2) if slots else (size // 4, 2, 2)
        return grad.reshape(lead + (grad.shape[0] // size,) + grad.shape[1:])

    codes = [rows[:, :letters] for rows in code_rows]
    conv_weight = own_blocks(merged_weight(kernels), 1)
    conv_shift = own_blocks(conv_bias, 0).astype(f32)
    forwards = [
        conv_forward(spread_letters(codes[0], character_table), code_rows[0][:, letters:], conv_weight, block)
    ]
    rows = hidden_in.shape[0]
    splits = hidden_out.shape[0] // rows
    inner_size = hidden_in.shape[1]
    turned_in = hidden_in.reshape(rows, size, splits, rows).transpose(0, 2, 1, 3).reshape(rows, inner_size)
    forward_shard = jnp.concatenate(
        [turned_in] + [hidden_out[part * rows : (part + 1) * rows] for part in range(splits)], axis=1
    )
    forward_all = lax.all_gather(after(forward_shard, forwards[0][0]), "dp", axis=0, tiled=True)
    inward_full = forward_all[:, :inner_size]
    outward_parts = [
        forward_all[:, inner_size + part * model : inner_size + (part + 1) * model] for part in range(splits)
    ]
    forwards.append(
        conv_forward(spread_letters(codes[1], character_table), code_rows[1][:, letters:], conv_weight, block)
    )
    biased = [forward[0] + conv_shift for forward in forwards]
    hidden0_parts = [jax.nn.relu(value) for value in biased]
    hidden0_low = [value.astype(low) for value in hidden0_parts]
    swapped = [seq_swap(value) for value in hidden0_low]
    hidden0_all = jnp.concatenate(
        [interleave(hidden0_low[0], swapped[1], piece), interleave(hidden0_low[1], swapped[0], piece)], axis=0
    )
    hidden0 = jnp.concatenate(hidden0_parts, axis=0)
    highway_shift = own_blocks(highway_bias.reshape(2, filters), 1).astype(f32)
    transform, gate = [
        jnp.dot(hidden0_all, highway_parts[part], preferred_element_type=f32) + highway_shift[part]
        for part in range(2)
    ]
    hidden1 = highway_mix(transform, gate, hidden0)
    hidden1_low = hidden1.astype(low)
    mapped = jnp.dot(hidden1_low, projection_full, preferred_element_type=f32)
    offset = side * words
    positions = lax.dynamic_slice_in_dim(position_table, offset, words, 0).astype(f32)
    embedded = mapped[:words] + seq_swap(mapped[words:].astype(low)).astype(f32) + positions
    embedded_low = embedded.astype(low)
    heads = model // HEAD_DIM
    projected = jnp.dot(embedded_low, attention_full, preferred_element_type=f32).astype(low)
    pairs = projected[:, model:]
    gathered = jnp.concatenate([pairs, seq_swap(pairs)], axis=0)
    length = gathered.shape[0]
    query_heads = projected[:, :model].reshape(words, heads, HEAD_DIM)
    key_heads = gathered[:, :model].reshape(length, heads, HEAD_DIM)
    value_heads = gathered[:, model:].reshape(length, heads, HEAD_DIM)
    keep = (jnp.arange(length, dtype=jnp.int32) + offset) % length < sequence_lengths[0]
    scores = score_heads(query_heads, key_heads, keep)
    top = jnp.max(scores, axis=-1, keepdims=True)
    unnormalized = jnp.exp(scores - top)
    total = jnp.sum(unnormalized, axis=-1, keepdims=True)
    probs_low = (unnormalized / total).astype(jnp.bfloat16)
    attended = jnp.einsum(
        "hqk,khd->qhd", probs_low, value_heads, preferred_element_type=jnp.float32
    )
    attended = attended.reshape(words, model).astype(jnp.bfloat16)
    joined = embedded + jnp.dot(attended, output_full, preferred_element_type=jnp.float32)
    gain1 = norm1_gain.astype(jnp.float32)
    shift1 = norm1_bias.astype(jnp.float32)
    gain2 = norm2_gain.astype(jnp.float32)
    shift2 = norm2_bias.astype(jnp.float32)
    normed1 = layer_norm(joined, gain1, shift1)
    normed1_low = normed1.astype(jnp.bfloat16)
    inner = jnp.dot(normed1_low, inward_full, preferred_element_type=jnp.float32)
    active = exact_gelu(inner).astype(jnp.bfloat16)
    actives = [active[:, part * model : (part + 1) * model] for part in range(splits)]
    summed = normed1 + sum(
        jnp.dot(actives[part], outward_parts[part], preferred_element_type=f32) for part in range(splits)
    )
    layer_out = layer_norm(summed, gain2, shift2).astype(jnp.bfloat16)
    seed_grad = cotangent[0].astype(jnp.float32)
    _, norm2_pull = jax.vjp(layer_norm, summed, gain2, shift2)
    grad_summed, norm2_gain_grad, norm2_bias_grad = norm2_pull(seed_grad)
    grad_outer = grad_summed.astype(jnp.bfloat16)
    hidden_out_grads = [
        jnp.einsum("tf,td->fd", part, grad_outer, preferred_element_type=f32).astype(low) for part in actives
    ]
    grad_active = jnp.concatenate(
        [jnp.einsum("td,fd->tf", grad_outer, part, preferred_element_type=f32) for part in outward_parts], axis=1
    )
    _, gelu_pull = jax.vjp(exact_gelu, inner)
    grad_inner = gelu_pull(grad_active)[0].astype(jnp.bfloat16)
    hidden_in_grad = jnp.einsum(
        "td,tf->df", normed1_low, grad_inner, preferred_element_type=jnp.float32
    ).astype(low)
    grad_normed1 = grad_summed + jnp.einsum(
        "tf,df->td", grad_inner, inward_full, preferred_element_type=jnp.float32
    )
    _, norm1_pull = jax.vjp(layer_norm, joined, gain1, shift1)
    grad_joined, norm1_gain_grad, norm1_bias_grad = norm1_pull(grad_normed1)
    forward_grad = jnp.concatenate([hidden_in_grad] + hidden_out_grads, axis=1)
    forward_sum = lax.psum_scatter(forward_grad, "dp", scatter_dimension=0, tiled=True)
    grad_branch = after(grad_joined.astype(low), forward_grad)
    attention_out_grad = jnp.einsum(
        "td,te->de", attended, grad_branch, preferred_element_type=jnp.float32
    ).astype(low)
    grad_attended = jnp.einsum(
        "te,de->td", grad_branch, output_full, preferred_element_type=jnp.float32
    ).astype(jnp.bfloat16)
    grad_heads = grad_attended.reshape(words, heads, HEAD_DIM)
    probs = jnp.exp(score_heads(query_heads, key_heads, keep) - top) / total
    probs_again = probs.astype(jnp.bfloat16)
    grad_probs = jnp.einsum(
        "qhd,khd->hqk", grad_heads, value_heads, preferred_element_type=jnp.float32
    )
    grad_scores = (
        probs * (grad_probs - jnp.sum(probs * grad_probs, axis=-1, keepdims=True))
    ).astype(jnp.bfloat16)
    grad_query = (
        jnp.einsum("hqk,khd->qhd", grad_scores, key_heads, preferred_element_type=jnp.float32)
        * 0.125
    )
    key_grad = (
        jnp.einsum("hqk,qhd->khd", grad_scores, query_heads, preferred_element_type=f32) * 0.125
    )
    value_grad = jnp.einsum("hqk,qhd->khd", probs_again, grad_heads, preferred_element_type=f32)
    pair_grads = jnp.concatenate(
        [key_grad.reshape(length, model), value_grad.reshape(length, model)], axis=1
    )
    pairs_lent = pair_grads[words:].astype(low)
    grad_pairs = pair_grads[:words] + seq_swap(pairs_lent).astype(f32)
    grad_projected = jnp.concatenate([grad_query.reshape(words, model), grad_pairs], axis=1).astype(low)
    attention_in_grad = jnp.einsum(
        "td,te->de", embedded_low, grad_projected, preferred_element_type=f32
    ).astype(low)
    grad_embedded = grad_joined + jnp.einsum(
        "te,de->td", grad_projected, attention_full, preferred_element_type=f32
    )
    grad_mapped = grad_embedded.astype(low)
    attention_half = scatter_core(cut(jnp.concatenate([attention_in_grad, attention_out_grad], axis=1)))
    grad_mapped = jnp.concatenate([grad_mapped, seq_swap(grad_mapped)], axis=0)
    grad_mapped = after(grad_mapped, attention_half)
    projection_grad = jnp.einsum(
        "tf,td->fd", hidden1_low, grad_mapped, preferred_element_type=f32
    ).astype(low)
    grad_hidden1 = jnp.einsum("td,fd->tf", grad_mapped, projection_full, preferred_element_type=f32)
    _, highway_pull = jax.vjp(highway_mix, transform, gate, hidden0)
    grad_transform, grad_gate, grad_carry = highway_pull(grad_hidden1)
    grad_gates = [grad_transform.astype(low), grad_gate.astype(low)]
    grad_spread = sum(
        jnp.einsum("tg,fg->tf", grad_gates[part], highway_parts[part], preferred_element_type=f32)
        for part in range(2)
    )
    grad_held, grad_lent = halves_of(grad_spread, piece)
    grad_lent = grad_lent.astype(low)
    lent_back = [seq_swap(grad_lent[words:]), seq_swap(grad_lent[:words])]
    grad_near = grad_carry + grad_held
    grad_pooled = [
        jnp.where(
            biased[part] > 0, grad_near[part * words : (part + 1) * words] + lent_back[part].astype(f32), 0.0
        )
        for part in range(2)
    ]
    highway_grads = [
        jnp.einsum("tf,tg->fg", hidden0_all, grad_gates[part], preferred_element_type=f32).astype(low)
        for part in range(2)
    ]
    highway_bias_grad = jnp.concatenate([jnp.sum(grad.astype(f32), axis=0) for grad in grad_gates])
    conv_bias_grad = jnp.sum(grad_pooled[0], axis=0) + jnp.sum(grad_pooled[1], axis=0)
    position_rows = 2 * words * model // mine // size
    position_low = grad_embedded.astype(low)
    nothing = jnp.zeros_like(position_low)
    position_grad = by_seq(position_low, nothing).reshape(size, position_rows, mine)
    highway_rows = jnp.concatenate(
        [highway_grads[0].reshape(size, piece, mine), position_grad], axis=1
    ).reshape(-1, mine)
    highway_sum = lax.psum_scatter(
        after(highway_rows, forward_sum), "dp", scatter_dimension=0, tiled=True
    )
    joint_half = scatter_core(
        cut(jnp.concatenate([highway_grads[1], projection_grad.reshape(filters, model // 2)], axis=1))
    )
    attention_quarter = scatter_middle(attention_half)
    joint_quarter = scatter_middle(joint_half)
    attention_sum = scatter_outer(attention_quarter)
    turned = conv_weight.T
    shares = [grad_pooled[part] / forwards[part][1] for part in range(2)]
    code_blocks = [
        codes[part].reshape(steps, block, letters).transpose(0, 2, 1).reshape(steps, 1, letters * block)
        for part in range(2)
    ]

    def back(part, first, count, *others):
        return conv_backward(
            forwards[part][2],
            forwards[part][3],
            code_blocks[part],
            conv_weight,
            turned,
            forwards[part][0],
            after(shares[part], *others),
            vocab,
            block,
            first,
            count,
        )

    cuts = steps // 2
    backs = [back(0, 0, cuts, attention_quarter, joint_half)]
    backs.append(back(0, cuts, steps - cuts, *backs[0]))
    backs.append(back(1, 0, cuts, attention_sum, joint_quarter, *backs[1]))
    joint_sum = scatter_outer(joint_quarter)
    backs.append(back(1, cuts, steps - cuts, *backs[2]))
    merged_grad = backs[0][0] + backs[1][0] + backs[2][0] + backs[3][0]
    table_wide = backs[0][1] + backs[1][1] + backs[2][1] + backs[3][1]
    table_grad = sum(
        table_wide[:vocab, shift * features : (shift + 1) * features] for shift in range(WIDTHS)
    )

    forward_total = seq_sum(forward_sum.astype(f32))
    inward_total = (
        forward_total[:, :inner_size].reshape(rows, splits, size, rows).transpose(0, 2, 1, 3).reshape(rows, inner_size)
    )
    outward_total = jnp.concatenate(
        [forward_total[:, inner_size + part * model : inner_size + (part + 1) * model] for part in range(splits)],
        axis=0,
    )
    attention_both = seq_sum(attention_sum)
    attention_total = attention_both[:, : 3 * model]
    output_total = attention_both[:, 3 * model :]
    part0 = highway_sum[:piece]
    position_part = highway_sum[piece:]
    position_part = (position_part.astype(f32) + seq_swap(position_part).astype(f32)).astype(low)
    part1 = joint_sum.astype(low)
    projection_part = part1[:, mine:].reshape(half, model)
    projection_pair = core_swap(projection_part)
    projection_sum = jnp.concatenate(
        [
            jnp.where(core == 0, projection_part, projection_pair),
            jnp.where(core == 0, projection_pair, projection_part),
        ],
        axis=0,
    )
    finals = jnp.concatenate([part0, part1[:, :mine], projection_sum], axis=1)
    finals_other = seq_swap(finals)
    projection_total = jnp.where(core == side, finals[:, 2 * mine :], finals_other[:, 2 * mine :]).astype(f32)
    highway_total = (
        by_seq(
            finals[:, : 2 * mine].reshape(piece, 2, chips, piece),
            finals_other[:, : 2 * mine].reshape(piece, 2, chips, piece),
        )
        .transpose(1, 2, 3, 0, 4)
        .reshape(piece, 2 * filters)
        .astype(f32)
    )

    conv_rows = WIDTHS * features
    table_rows = -(-vocab * features // mine)
    table_flat = jnp.pad(table_grad.reshape(-1), (0, table_rows * mine - vocab * features))
    entries = [
        merged_grad[:conv_rows],
        conv_bias_grad[None],
        highway_bias_grad.reshape(2, mine),
        table_flat.reshape(table_rows, mine),
        jnp.concatenate([norm1_gain_grad, norm1_bias_grad, norm2_gain_grad, norm2_bias_grad]).reshape(-1, mine),
    ]
    starts = [0]
    for row in entries:
        starts.append(starts[-1] + row.shape[0])
    padded = -(-starts[-1] // size) * size
    small = jnp.pad(jnp.concatenate(entries, axis=0), ((0, padded - starts[-1]), (0, 0)))
    small = after(small, joint_sum, attention_both)
    small = scatter_outer(scatter_middle(scatter_core(cut(small)))).astype(low)
    share = small.shape[0]
    small = jnp.concatenate([small, seq_swap(small), position_part], axis=0)
    near = gather_near(outer_pieces(small))
    across = middle_swap(near)
    small = gather((near, across, core_swap(near), core_swap(across))).reshape(size, -1, mine)
    small_own = small[:, :share].reshape(padded, mine)
    small_other = small[:, share : 2 * share].reshape(padded, mine)
    own = [small_own[starts[i] : starts[i + 1]] for i in range(len(entries))]
    other = [small_other[starts[i] : starts[i + 1]] for i in range(len(entries))]
    conv_all = (
        by_seq(own[0].reshape(conv_rows, chips, piece), other[0].reshape(conv_rows, chips, piece))
        .transpose(1, 2, 0, 3)
        .reshape(conv_rows, filters)
        .astype(f32)
    )
    conv_bias_total = (
        by_seq(own[1].reshape(chips, piece), other[1].reshape(chips, piece))
        .transpose(1, 0, 2)
        .reshape(filters)
        .astype(f32)
    )
    highway_bias_total = (
        by_seq(own[2].reshape(2, chips, piece), other[2].reshape(2, chips, piece))
        .transpose(1, 2, 0, 3)
        .reshape(2 * filters)
        .astype(f32)
    )
    table_total = (own[3].astype(f32) + other[3].astype(f32)).reshape(-1)
    table_total = table_total[: vocab * features].reshape(vocab, features)
    norms = (own[4].astype(f32) + other[4].astype(f32)).reshape(4, model)
    position_total = small[:, 2 * share :].reshape(2 * words, model).astype(f32)
    kernel_grads = []
    first = 0
    for kernel in kernels:
        kernel_grads.append(conv_all[: kernel.shape[0], first : first + kernel.shape[1]])
        first = first + kernel.shape[1]
    return (
        layer_out[None],
        table_total,
        *kernel_grads,
        conv_bias_total,
        highway_total,
        highway_bias_total,
        projection_total,
        position_total,
        attention_total,
        output_total,
        norms[0],
        norms[1],
        inward_total,
        outward_total,
        norms[2],
        norms[3],
    )


def solution(mesh):
    placed = (
        P("dp", "seq", None),
        P("dp", "seq"),
        P("dp"),
        P(),
        P(),
        P(),
        P(),
        P(),
        P(),
        P(),
        P(),
        P(),
        P("dp", None),
        P(),
        P("dp", None),
        P(),
        P("dp", None),
        P("dp", None),
        P(),
        P(),
        P("dp", None),
        P("dp", None),
        P(),
        P(),
        P("dp", "seq", None),
    )
    return jax.shard_map(
        body,
        mesh=mesh,
        in_specs=placed,
        out_specs=(
            P("dp", "seq", None),
            P(),
            P(),
            P(),
            P(),
            P(),
            P(),
            P(),
            P(),
            P(),
            P("dp", None),
            P(),
            P("dp", None),
            P(),
            P("dp", None),
            P("dp", None),
            P(),
            P(),
            P("dp", None),
            P("dp", None),
            P(),
            P(),
        ),
        check_vma=False,
    )
```

```python
from functools import partial
import math

import jax
import jax.numpy as jnp
from jax import lax
from jax.experimental import pallas as pl
from jax.experimental.pallas import tpu as pltpu
from jax.sharding import PartitionSpec as P

HEAD_DIM = 64


exact_gelu = partial(jax.nn.gelu, approximate=False)


def layer_norm(value, gain, bias):
    mean = jnp.mean(value, axis=-1, keepdims=True)
    centered = value - mean
    spread = jnp.mean(centered * centered, axis=-1, keepdims=True)
    return centered * lax.rsqrt(spread + 1e-12) * gain + bias


def highway_mix(transform, gate, hidden):
    carry = jax.nn.sigmoid(gate)
    return carry * hidden + (1.0 - carry) * jax.nn.relu(transform)


def place():
    spot = lax.axis_index("dp")
    return (spot // 4, (spot // 2) % 2, spot % 2)


def core_swap(value):
    size = lax.axis_size("dp")
    return lax.ppermute(value, "dp", [(spot, spot ^ 1) for spot in range(size)])


def middle_swap(value):
    size = lax.axis_size("dp")
    return lax.ppermute(value, "dp", [(spot, spot ^ 2) for spot in range(size)])


def outer_shift(value, steps):
    size = lax.axis_size("dp")
    return lax.ppermute(value, "dp", [(spot, (spot - 4 * steps) % size) for spot in range(size)])


def seq_swap(value):
    return lax.ppermute(value, "seq", [(0, 1), (1, 0)])


def after(value, *others):
    return lax.optimization_barrier((value,) + others)[0]


def pick(value, index, axis):
    return lax.dynamic_index_in_dim(value, index, axis, keepdims=False)


def outer_pieces(shard):
    return [shard] + [outer_shift(shard, steps) for steps in range(1, lax.axis_size("dp") // 4)]


def gather_near(pieces):
    outer = place()[0]
    size = len(pieces)
    near = jnp.zeros((size,) + pieces[0].shape, pieces[0].dtype)
    for steps, piece in enumerate(pieces):
        near = lax.dynamic_update_index_in_dim(near, piece, (outer + steps) % size, 0)
    return near


def gather(values, side=None):
    _, middle, core = place()
    size = values[0].shape[0]
    shape = values[0].shape[1:]
    zeros = (0,) * len(shape)
    whole = jnp.zeros(((size, 2, 2) if side is None else (2, size, 2)) + shape, values[0].dtype)
    for flip, value in enumerate(values):
        flip_middle, flip_core = flip % 2, flip // 2
        if side is None:
            start = (0, middle ^ flip_middle, core ^ flip_core) + zeros
            value = value[:, None, None]
        else:
            start = (core ^ side ^ flip_core, 0, middle ^ flip_middle) + zeros
            value = value[None, :, None]
        whole = lax.dynamic_update_slice(whole, value, start)
    return whole


def scatter_core(parts, side=None):
    _, _, core = place()
    axis, slot = (2, core) if side is None else (0, core ^ side)
    other = core_swap(pick(parts, 1 - slot, axis).astype(jnp.bfloat16))
    return pick(parts, slot, axis).astype(jnp.float32) + other.astype(jnp.float32)


def scatter_middle(half, first=(), last=()):
    _, middle, _ = place()
    sent = after(pick(half, 1 - middle, 1).astype(jnp.bfloat16), *first)
    return pick(half, middle, 1) + after(middle_swap(sent), *last).astype(jnp.float32)


def scatter_outer(quarter, first=(), last=()):
    outer, _, _ = place()
    size = quarter.shape[0]
    rounded = after(quarter.astype(jnp.bfloat16), *first)
    pieces = [
        outer_shift(pick(rounded, (outer + size - steps) % size, 0), steps) for steps in range(1, size)
    ]
    if last:
        pieces = lax.optimization_barrier(tuple(pieces) + tuple(last))[: size - 1]
    total = pick(quarter, outer, 0)
    for value in pieces:
        total = total + value.astype(jnp.float32)
    return total


def seq_sum(value):
    return value + seq_swap(value.astype(jnp.bfloat16)).astype(jnp.float32)


def own_blocks(value, axis):
    axis = axis % value.ndim
    size = lax.axis_size("dp")
    shape = value.shape
    split = shape[:axis] + (size // 2, 2, shape[axis] // size) + shape[axis + 1 :]
    chosen = pick(value.reshape(split), lax.axis_index("seq"), axis + 1)
    return chosen.reshape(shape[:axis] + (shape[axis] // 2,) + shape[axis + 1 :])


def interleave(own, other, piece):
    first = lax.axis_index("seq") == 0
    blocks = []
    for start in range(0, own.shape[1], piece):
        mine, theirs = own[:, start : start + piece], other[:, start : start + piece]
        blocks += [jnp.where(first, mine, theirs), jnp.where(first, theirs, mine)]
    return jnp.concatenate(blocks, axis=1)


def halves_of(value, piece):
    first = lax.axis_index("seq") == 0
    own, other = [], []
    for start in range(0, value.shape[1], 2 * piece):
        even, odd = value[:, start : start + piece], value[:, start + piece : start + 2 * piece]
        own.append(jnp.where(first, even, odd))
        other.append(jnp.where(first, odd, even))
    return jnp.concatenate(own, axis=1), jnp.concatenate(other, axis=1)


def by_seq(own, other):
    first = lax.axis_index("seq") == 0
    return jnp.stack([jnp.where(first, own, other), jnp.where(first, other, own)])


WIDTHS = 7
LANES = 128
NEG = -1e30


def conv_forward_kernel(spread_ref, lens_ref, weight_ref, pooled_ref, ties_ref, window_ref, flipped_ref, scores_ref):
    letters, words, _ = spread_ref.shape
    channels = weight_ref.shape[1]
    lane = lax.broadcasted_iota(jnp.int32, (words, LANES), 1)
    slot = lane // 16
    limit = jnp.maximum(lens_ref[...] - (lane - 16 * WIDTHS), 1)
    for p in range(letters):
        window = jnp.zeros((words, LANES), jnp.float32)
        for j in range(WIDTHS):
            if p + j < letters:
                window = jnp.where(slot == j, spread_ref[p + j].astype(jnp.float32), window)
        flag = jnp.where((lane >= 16 * WIDTHS) & (lane < 17 * WIDTHS) & (p >= limit), 1.0, window)
        window_ref[p * words:(p + 1) * words] = flag.astype(jnp.bfloat16)
    flipped_ref[...] = window_ref[...].T
    tile = 256

    def one_tile(index, _):
        c = pl.multiple_of(index * tile, tile)
        scores_ref[...] = jnp.dot(window_ref[...], weight_ref[:, pl.ds(c, tile)], preferred_element_type=jnp.float32)
        for r in range(0, words, 16):
            top = scores_ref[r:r + 16]
            for p in range(1, letters):
                top = jnp.maximum(top, scores_ref[p * words + r:p * words + r + 16])
            count = jnp.zeros((16, tile), jnp.float32)
            for p in range(letters):
                count += jnp.where(scores_ref[p * words + r:p * words + r + 16] == top, 1.0, 0.0)
            pooled_ref[r:r + 16, pl.ds(c, tile)] = top
            ties_ref[r:r + 16, pl.ds(c, tile)] = count
        return 0

    lax.fori_loop(0, channels // tile, one_tile, 0)


def conv_backward_kernel(window_ref, flipped_ref, codes_ref, weight_ref, turned_ref, pooled_ref, share_in_ref,
                         grad_ref, table_ref, share_ref, scores_ref, spread_ref, letters):
    rows = window_ref.shape[0]
    words = rows // letters
    channels = weight_ref.shape[1]
    vocab = table_ref.shape[0]
    tile = 256

    @pl.when(pl.program_id(0) == 0)
    def _():
        grad_ref[...] = jnp.zeros_like(grad_ref)
        table_ref[...] = jnp.zeros_like(table_ref)

    def one_tile(index, _):
        c = pl.multiple_of(index * tile, tile)
        scores_ref[...] = jnp.dot(window_ref[...], weight_ref[:, pl.ds(c, tile)], preferred_element_type=jnp.float32)
        for r in range(0, words, 16):
            top = pooled_ref[r:r + 16, pl.ds(c, tile)]
            part = share_in_ref[r:r + 16, pl.ds(c, tile)]
            for p in range(letters):
                hit = scores_ref[p * words + r:p * words + r + 16] == top
                share_ref[p * words + r:p * words + r + 16, pl.ds(c, tile)] = jnp.where(hit, part, 0.0).astype(jnp.bfloat16)
        return 0

    lax.fori_loop(0, channels // tile, one_tile, 0)
    grad_ref[...] += jnp.dot(flipped_ref[...], share_ref[...], preferred_element_type=jnp.float32)
    scores_ref[:, :LANES] = jnp.dot(share_ref[...], turned_ref[...], preferred_element_type=jnp.float32)
    slot = lax.broadcasted_iota(jnp.int32, (words, LANES), 1) // 16
    for c in range(letters):
        spread = jnp.zeros((words, LANES), jnp.float32)
        for j in range(WIDTHS):
            if c - j >= 0:
                spread = jnp.where(slot == j, scores_ref[(c - j) * words:(c - j + 1) * words, :LANES], spread)
        spread_ref[c * words:(c + 1) * words] = spread.astype(jnp.bfloat16)
    onehot = jnp.where(lax.broadcasted_iota(jnp.int32, (vocab, rows), 0) == codes_ref[0], 1.0, 0.0).astype(jnp.bfloat16)
    table_ref[...] += jnp.dot(onehot, spread_ref[...], preferred_element_type=jnp.float32)


def conv_forward(spread, lens, weight, block):
    letters, words, _ = spread.shape
    channels = weight.shape[1]
    steps = words // block
    rows = letters * block
    f32 = jnp.float32
    return pl.pallas_call(
        conv_forward_kernel,
        grid=(steps,),
        in_specs=[
            pl.BlockSpec((letters, block, LANES), lambda i: (0, i, 0)),
            pl.BlockSpec((block, 1), lambda i: (i, 0)),
            pl.BlockSpec((LANES, channels), lambda i: (0, 0)),
        ],
        out_specs=[
            pl.BlockSpec((block, channels), lambda i: (i, 0)),
            pl.BlockSpec((block, channels), lambda i: (i, 0)),
            pl.BlockSpec((rows, LANES), lambda i: (i, 0)),
            pl.BlockSpec((LANES, rows), lambda i: (0, i)),
        ],
        out_shape=[
            jax.ShapeDtypeStruct((words, channels), f32),
            jax.ShapeDtypeStruct((words, channels), f32),
            jax.ShapeDtypeStruct((steps * rows, LANES), jnp.bfloat16),
            jax.ShapeDtypeStruct((LANES, steps * rows), jnp.bfloat16),
        ],
        scratch_shapes=[pltpu.VMEM((rows, 256), f32)],
        compiler_params=pltpu.CompilerParams(dimension_semantics=("arbitrary",)),
        cost_estimate=pl.CostEstimate(
            flops=2 * LANES * steps * rows * channels,
            bytes_accessed=steps * rows * channels * 5,
            transcendentals=0,
        ),
        name="conv_forward",
    )(spread, lens, weight)


def conv_backward(window, flipped, codes, weight, turned, pooled, share, vocab, block, first, steps):
    words, channels = pooled.shape
    rows = window.shape[0] // (words // block)
    letters = rows // block
    f32 = jnp.float32
    vocab = -(-vocab // 16) * 16

    def kernel(*refs):
        conv_backward_kernel(*refs, letters=letters)

    return pl.pallas_call(
        kernel,
        grid=(steps,),
        in_specs=[
            pl.BlockSpec((rows, LANES), lambda i: (first + i, 0)),
            pl.BlockSpec((LANES, rows), lambda i: (0, first + i)),
            pl.BlockSpec((1, 1, rows), lambda i: (first + i, 0, 0)),
            pl.BlockSpec((LANES, channels), lambda i: (0, 0)),
            pl.BlockSpec((channels, LANES), lambda i: (0, 0)),
            pl.BlockSpec((block, channels), lambda i: (first + i, 0)),
            pl.BlockSpec((block, channels), lambda i: (first + i, 0)),
        ],
        out_specs=[
            pl.BlockSpec((LANES, channels), lambda i: (0, 0)),
            pl.BlockSpec((vocab, LANES), lambda i: (0, 0)),
        ],
        out_shape=[
            jax.ShapeDtypeStruct((LANES, channels), f32),
            jax.ShapeDtypeStruct((vocab, LANES), f32),
        ],
        scratch_shapes=[
            pltpu.VMEM((rows, channels), jnp.bfloat16),
            pltpu.VMEM((rows, 256), f32),
            pltpu.VMEM((rows, LANES), jnp.bfloat16),
        ],
        compiler_params=pltpu.CompilerParams(dimension_semantics=("arbitrary",)),
        cost_estimate=pl.CostEstimate(
            flops=6 * LANES * steps * rows * channels,
            bytes_accessed=steps * rows * channels * 8,
            transcendentals=0,
        ),
        name="conv_backward",
    )(window, flipped, codes, weight, turned, pooled, share)


def merge_kernel(*refs):
    whole_ref = refs[-1]
    whole_ref[...] = jnp.zeros_like(whole_ref)
    features = refs[0].shape[0]
    first = 0
    for width, kernel_ref in enumerate(refs[:-1], 1):
        channels = kernel_ref.shape[1]
        whole_ref[: width * features, first : first + channels] = kernel_ref[...]
        marks = lax.broadcasted_iota(jnp.int32, (16, channels), 0) == width - 1
        whole_ref[WIDTHS * features :, first : first + channels] = jnp.where(marks, NEG, 0.0).astype(jnp.bfloat16)
        first = first + channels


def merged_weight(kernels):
    channels = sum(kernel.shape[1] for kernel in kernels)
    return pl.pallas_call(
        merge_kernel, out_shape=jax.ShapeDtypeStruct((LANES, channels), jnp.bfloat16), name="merge_widths"
    )(*kernels)


def spread_letters(codes, table):
    vocab, features = table.shape
    words, letters = codes.shape
    wide = jnp.tile(table, (1, LANES // features))
    onehot = (codes.T.reshape(-1, 1) == jnp.arange(vocab, dtype=jnp.int32)[None, :]).astype(jnp.bfloat16)
    return jnp.dot(onehot, wide, preferred_element_type=jnp.float32).astype(jnp.bfloat16).reshape(letters, words, LANES)


def score_heads(query_heads, key_heads, keep):
    raw = (
        jnp.einsum("qhd,khd->hqk", query_heads, key_heads, preferred_element_type=jnp.float32)
        * 0.125
    )
    return jnp.where(keep[None, None, :], raw, -1e30)


def body(
    character_codes,
    word_lengths,
    sequence_lengths,
    character_table,
    conv_width1,
    conv_width2,
    conv_width3,
    conv_width4,
    conv_width5,
    conv_width6,
    conv_width7,
    conv_bias,
    highway_weight,
    highway_bias,
    projection,
    position_table,
    attention_in,
    attention_out,
    norm1_gain,
    norm1_bias,
    hidden_in,
    hidden_out,
    norm2_gain,
    norm2_bias,
    cotangent,
):
    kernels = (
        conv_width1,
        conv_width2,
        conv_width3,
        conv_width4,
        conv_width5,
        conv_width6,
        conv_width7,
    )
    f32 = jnp.float32
    low = jnp.bfloat16
    side = lax.axis_index("seq")
    outer, middle, core = place()
    size = lax.axis_size("dp")
    chips = size // 2
    words = character_codes.shape[1]
    letters = character_codes.shape[2]
    vocab, features = character_table.shape
    filters = conv_bias.shape[0]
    mine = filters // 2
    piece = filters // size
    half = piece // 2
    model = position_table.shape[1]
    block = math.gcd(words, 64)
    steps = words // block

    highway_shard = own_blocks(highway_weight.reshape(-1, 2, filters), 2)
    held = lax.dynamic_slice_in_dim(projection, core * half, half, 0)
    lent = lax.dynamic_slice_in_dim(projection, (1 - core) * half, half, 0)
    projection_shard = jnp.where(core == side, held, core_swap(lent))
    code_rows = jnp.concatenate([character_codes[0], word_lengths[0][:, None]], axis=1)
    code_rows = [code_rows, seq_swap(code_rows)]

    joint_shard = jnp.concatenate(
        [highway_shard.reshape(piece, filters), projection_shard.reshape(piece, model // 2)], axis=1
    )
    joint_all = lax.all_gather(joint_shard, "dp", axis=0, tiled=True)
    highway_parts = [joint_all[:, :mine], joint_all[:, mine:filters]]
    projection_full = joint_all[:, filters:].reshape(mine, model)
    attention_near = gather_near(outer_pieces(jnp.concatenate([attention_in, attention_out], axis=1)))
    attention_across = middle_swap(attention_near)
    attention_far = [core_swap(attention_near), core_swap(attention_across)]
    attention_all = gather((attention_near, attention_across, *attention_far)).reshape(model, -1)
    attention_full = attention_all[:, : 3 * model]
    output_full = attention_all[:, 3 * model :]

    def cut(grad, slots=False):
        lead = (2, size // 4, 2) if slots else (size // 4, 2, 2)
        return grad.reshape(lead + (grad.shape[0] // size,) + grad.shape[1:])

    codes = [rows[:, :letters] for rows in code_rows]
    conv_weight = own_blocks(merged_weight(kernels), 1)
    conv_shift = own_blocks(conv_bias, 0).astype(f32)
    forwards = [
        conv_forward(spread_letters(codes[0], character_table), code_rows[0][:, letters:], conv_weight, block)
    ]
    rows = hidden_in.shape[0]
    splits = hidden_out.shape[0] // rows
    inner_size = hidden_in.shape[1]
    turned_in = hidden_in.reshape(rows, size, splits, rows).transpose(0, 2, 1, 3).reshape(rows, inner_size)
    forward_shard = jnp.concatenate(
        [turned_in] + [hidden_out[part * rows : (part + 1) * rows] for part in range(splits)], axis=1
    )
    forward_all = lax.all_gather(after(forward_shard, forwards[0][0]), "dp", axis=0, tiled=True)
    inward_full = forward_all[:, :inner_size]
    outward_parts = [
        forward_all[:, inner_size + part * model : inner_size + (part + 1) * model] for part in range(splits)
    ]
    forwards.append(
        conv_forward(spread_letters(codes[1], character_table), code_rows[1][:, letters:], conv_weight, block)
    )
    biased = [forward[0] + conv_shift for forward in forwards]
    hidden0_parts = [jax.nn.relu(value) for value in biased]
    hidden0_low = [value.astype(low) for value in hidden0_parts]
    swapped = [seq_swap(value) for value in hidden0_low]
    hidden0_all = jnp.concatenate(
        [interleave(hidden0_low[0], swapped[1], piece), interleave(hidden0_low[1], swapped[0], piece)], axis=0
    )
    hidden0 = jnp.concatenate(hidden0_parts, axis=0)
    highway_shift = own_blocks(highway_bias.reshape(2, filters), 1).astype(f32)
    transform, gate = [
        jnp.dot(hidden0_all, highway_parts[part], preferred_element_type=f32) + highway_shift[part]
        for part in range(2)
    ]
    hidden1 = highway_mix(transform, gate, hidden0)
    hidden1_low = hidden1.astype(low)
    mapped = jnp.dot(hidden1_low, projection_full, preferred_element_type=f32)
    offset = side * words
    positions = lax.dynamic_slice_in_dim(position_table, offset, words, 0).astype(f32)
    embedded = mapped[:words] + seq_swap(mapped[words:].astype(low)).astype(f32) + positions
    embedded_low = embedded.astype(low)
    heads = model // HEAD_DIM
    projected = jnp.dot(embedded_low, attention_full, preferred_element_type=f32).astype(low)
    gathered = jnp.concatenate(
        [
            jnp.concatenate([pair, seq_swap(pair)], axis=0)
            for pair in (projected[:, model : 2 * model], projected[:, 2 * model :])
        ],
        axis=1,
    )
    length = gathered.shape[0]
    query_heads = projected[:, :model].reshape(words, heads, HEAD_DIM)
    key_heads = gathered[:, :model].reshape(length, heads, HEAD_DIM)
    value_heads = gathered[:, model:].reshape(length, heads, HEAD_DIM)
    keep = (jnp.arange(length, dtype=jnp.int32) + offset) % length < sequence_lengths[0]
    scores = score_heads(query_heads, key_heads, keep)
    top = jnp.max(scores, axis=-1, keepdims=True)
    unnormalized = jnp.exp(scores - top)
    total = jnp.sum(unnormalized, axis=-1, keepdims=True)
    probs_low = (unnormalized / total).astype(jnp.bfloat16)
    attended = jnp.einsum(
        "hqk,khd->qhd", probs_low, value_heads, preferred_element_type=jnp.float32
    )
    attended = attended.reshape(words, model).astype(jnp.bfloat16)
    joined = embedded + jnp.dot(attended, output_full, preferred_element_type=jnp.float32)
    gain1 = norm1_gain.astype(jnp.float32)
    shift1 = norm1_bias.astype(jnp.float32)
    gain2 = norm2_gain.astype(jnp.float32)
    shift2 = norm2_bias.astype(jnp.float32)
    normed1 = layer_norm(joined, gain1, shift1)
    normed1_low = normed1.astype(jnp.bfloat16)
    inner = jnp.dot(normed1_low, inward_full, preferred_element_type=jnp.float32)
    active = exact_gelu(inner).astype(jnp.bfloat16)
    actives = [active[:, part * model : (part + 1) * model] for part in range(splits)]
    summed = normed1 + sum(
        jnp.dot(actives[part], outward_parts[part], preferred_element_type=f32) for part in range(splits)
    )
    layer_out = layer_norm(summed, gain2, shift2).astype(jnp.bfloat16)
    seed_grad = cotangent[0].astype(jnp.float32)
    _, norm2_pull = jax.vjp(layer_norm, summed, gain2, shift2)
    grad_summed, norm2_gain_grad, norm2_bias_grad = norm2_pull(seed_grad)
    grad_outer = grad_summed.astype(jnp.bfloat16)
    hidden_out_grads = [
        jnp.einsum("tf,td->fd", part, grad_outer, preferred_element_type=f32).astype(low) for part in actives
    ]
    grad_active = jnp.concatenate(
        [jnp.einsum("td,fd->tf", grad_outer, part, preferred_element_type=f32) for part in outward_parts], axis=1
    )
    _, gelu_pull = jax.vjp(exact_gelu, inner)
    grad_inner = gelu_pull(grad_active)[0].astype(jnp.bfloat16)
    hidden_in_grad = jnp.einsum(
        "td,tf->df", normed1_low, grad_inner, preferred_element_type=jnp.float32
    ).astype(low)
    grad_normed1 = grad_summed + jnp.einsum(
        "tf,df->td", grad_inner, inward_full, preferred_element_type=jnp.float32
    )
    _, norm1_pull = jax.vjp(layer_norm, joined, gain1, shift1)
    grad_joined, norm1_gain_grad, norm1_bias_grad = norm1_pull(grad_normed1)
    forward_grad = jnp.concatenate([hidden_in_grad] + hidden_out_grads, axis=1)
    forward_sum = lax.psum_scatter(forward_grad, "dp", scatter_dimension=0, tiled=True)
    grad_branch = after(grad_joined.astype(low), forward_grad)
    attention_out_grad = jnp.einsum(
        "td,te->de", attended, grad_branch, preferred_element_type=jnp.float32
    ).astype(low)
    grad_attended = jnp.einsum(
        "te,de->td", grad_branch, output_full, preferred_element_type=jnp.float32
    ).astype(jnp.bfloat16)
    grad_heads = grad_attended.reshape(words, heads, HEAD_DIM)
    probs = jnp.exp(score_heads(query_heads, key_heads, keep) - top) / total
    probs_again = probs.astype(jnp.bfloat16)
    value_grad = jnp.einsum("hqk,qhd->khd", probs_again, grad_heads, preferred_element_type=f32)
    grad_probs = jnp.einsum(
        "qhd,khd->hqk", grad_heads, value_heads, preferred_element_type=jnp.float32
    )
    grad_scores = (
        probs * (grad_probs - jnp.sum(probs * grad_probs, axis=-1, keepdims=True))
    ).astype(jnp.bfloat16)
    grad_query = (
        jnp.einsum("hqk,khd->qhd", grad_scores, key_heads, preferred_element_type=jnp.float32)
        * 0.125
    )
    key_grad = (
        jnp.einsum("hqk,qhd->khd", grad_scores, query_heads, preferred_element_type=f32) * 0.125
    )
    value_grad = value_grad.reshape(length, model)
    key_grad = key_grad.reshape(length, model)
    value_back = seq_swap(value_grad[words:].astype(low))
    key_back = seq_swap(key_grad[words:].astype(low))
    grad_pairs = jnp.concatenate(
        [key_grad[:words] + key_back.astype(f32), value_grad[:words] + value_back.astype(f32)], axis=1
    )
    grad_projected = jnp.concatenate([grad_query.reshape(words, model), grad_pairs], axis=1).astype(low)
    attention_in_grad = jnp.einsum(
        "td,te->de", embedded_low, grad_projected, preferred_element_type=f32
    ).astype(low)
    grad_embedded = grad_joined + jnp.einsum(
        "te,de->td", grad_projected, attention_full, preferred_element_type=f32
    )
    grad_mapped = grad_embedded.astype(low)
    attention_half = scatter_core(cut(jnp.concatenate([attention_in_grad, attention_out_grad], axis=1)))
    grad_mapped = jnp.concatenate([grad_mapped, seq_swap(grad_mapped)], axis=0)
    grad_mapped = after(grad_mapped, attention_half)
    projection_grad = jnp.einsum(
        "tf,td->fd", hidden1_low, grad_mapped, preferred_element_type=f32
    ).astype(low)
    grad_hidden1 = jnp.einsum("td,fd->tf", grad_mapped, projection_full, preferred_element_type=f32)
    _, highway_pull = jax.vjp(highway_mix, transform, gate, hidden0)
    grad_transform, grad_gate, grad_carry = highway_pull(grad_hidden1)
    grad_gates = [grad_transform.astype(low), grad_gate.astype(low)]
    grad_spread = sum(
        jnp.einsum("tg,fg->tf", grad_gates[part], highway_parts[part], preferred_element_type=f32)
        for part in range(2)
    )
    grad_held, grad_lent = halves_of(grad_spread, piece)
    grad_lent = grad_lent.astype(low)
    lent_back = [seq_swap(grad_lent[words:]), seq_swap(grad_lent[:words])]
    grad_near = grad_carry + grad_held
    grad_pooled = [
        jnp.where(
            biased[part] > 0, grad_near[part * words : (part + 1) * words] + lent_back[part].astype(f32), 0.0
        )
        for part in range(2)
    ]
    highway_grads = [
        jnp.einsum("tf,tg->fg", hidden0_all, grad_gates[part], preferred_element_type=f32).astype(low)
        for part in range(2)
    ]
    highway_bias_grad = jnp.concatenate([jnp.sum(grad.astype(f32), axis=0) for grad in grad_gates])
    conv_bias_grad = jnp.sum(grad_pooled[0], axis=0) + jnp.sum(grad_pooled[1], axis=0)
    position_rows = 2 * words * model // mine // size
    position_low = grad_embedded.astype(low)
    nothing = jnp.zeros_like(position_low)
    position_grad = by_seq(position_low, nothing).reshape(size, position_rows, mine)
    highway_rows = jnp.concatenate(
        [highway_grads[0].reshape(size, piece, mine), position_grad], axis=1
    ).reshape(-1, mine)
    highway_sum = lax.psum_scatter(
        after(highway_rows, forward_sum), "dp", scatter_dimension=0, tiled=True
    )
    joint_half = scatter_core(
        cut(jnp.concatenate([highway_grads[1], projection_grad.reshape(filters, model // 2)], axis=1))
    )
    attention_quarter = scatter_middle(attention_half)
    turned = conv_weight.T
    shares = [grad_pooled[part] / forwards[part][1] for part in range(2)]
    code_blocks = [
        codes[part].reshape(steps, block, letters).transpose(0, 2, 1).reshape(steps, 1, letters * block)
        for part in range(2)
    ]

    def back(part, first, count, *others):
        return conv_backward(
            forwards[part][2],
            forwards[part][3],
            code_blocks[part],
            conv_weight,
            turned,
            forwards[part][0],
            after(shares[part], *others),
            vocab,
            block,
            first,
            count,
        )

    cuts = steps // 2
    backs = [back(0, 0, cuts, attention_quarter, joint_half, highway_rows)]
    attention_sum = scatter_outer(attention_quarter, grad_pooled, backs[0])
    joint_quarter = scatter_middle(joint_half, grad_pooled, backs[0])
    backs.append(back(0, cuts, steps - cuts, attention_sum, joint_quarter, *backs[0]))
    forward_both = forward_sum.astype(f32) + after(seq_swap(after(forward_sum, *backs[0])), *backs[1]).astype(f32)
    backs.append(back(1, 0, cuts, forward_sum, *backs[1]))
    attention_both = attention_sum + after(seq_swap(after(attention_sum.astype(low), *backs[1])), *backs[2]).astype(f32)
    backs.append(back(1, cuts, steps - cuts, forward_both, *backs[2]))
    joint_sum = scatter_outer(joint_quarter, backs[0], backs[3])
    merged_grad = backs[0][0] + backs[1][0] + backs[2][0] + backs[3][0]
    table_wide = backs[0][1] + backs[1][1] + backs[2][1] + backs[3][1]
    table_grad = sum(
        table_wide[:vocab, shift * features : (shift + 1) * features] for shift in range(WIDTHS)
    )

    forward_total = forward_both
    inward_total = (
        forward_total[:, :inner_size].reshape(rows, splits, size, rows).transpose(0, 2, 1, 3).reshape(rows, inner_size)
    )
    outward_total = jnp.concatenate(
        [forward_total[:, inner_size + part * model : inner_size + (part + 1) * model] for part in range(splits)],
        axis=0,
    )
    attention_total = attention_both[:, : 3 * model]
    output_total = attention_both[:, 3 * model :]
    part0 = highway_sum[:piece]
    position_part = highway_sum[piece:]
    position_part = (position_part.astype(f32) + seq_swap(position_part).astype(f32)).astype(low)
    part1 = joint_sum.astype(low)
    projection_part = part1[:, mine:].reshape(half, model)
    projection_pair = core_swap(projection_part)
    projection_sum = jnp.concatenate(
        [
            jnp.where(core == 0, projection_part, projection_pair),
            jnp.where(core == 0, projection_pair, projection_part),
        ],
        axis=0,
    )
    finals = jnp.concatenate([part0, part1[:, :mine], projection_sum], axis=1)
    finals_other = seq_swap(finals)
    projection_total = jnp.where(core == side, finals[:, 2 * mine :], finals_other[:, 2 * mine :]).astype(f32)
    highway_total = (
        by_seq(
            finals[:, : 2 * mine].reshape(piece, 2, chips, piece),
            finals_other[:, : 2 * mine].reshape(piece, 2, chips, piece),
        )
        .transpose(1, 2, 3, 0, 4)
        .reshape(piece, 2 * filters)
        .astype(f32)
    )

    conv_rows = WIDTHS * features
    table_rows = -(-vocab * features // mine)
    table_flat = jnp.pad(table_grad.reshape(-1), (0, table_rows * mine - vocab * features))
    entries = [
        merged_grad[:conv_rows],
        conv_bias_grad[None],
        highway_bias_grad.reshape(2, mine),
        table_flat.reshape(table_rows, mine),
        jnp.concatenate([norm1_gain_grad, norm1_bias_grad, norm2_gain_grad, norm2_bias_grad]).reshape(-1, mine),
    ]
    starts = [0]
    for row in entries:
        starts.append(starts[-1] + row.shape[0])
    padded = -(-starts[-1] // size) * size
    small = jnp.pad(jnp.concatenate(entries, axis=0), ((0, padded - starts[-1]), (0, 0)))
    small = after(small, joint_sum, attention_both, highway_sum)
    small = scatter_outer(scatter_middle(scatter_core(cut(small)))).astype(low)
    share = small.shape[0]
    small = after(jnp.concatenate([small, seq_swap(small), position_part], axis=0), finals_other)
    near = gather_near(outer_pieces(small))
    across = middle_swap(near)
    small = gather((near, across, core_swap(near), core_swap(across))).reshape(size, -1, mine)
    small_own = small[:, :share].reshape(padded, mine)
    small_other = small[:, share : 2 * share].reshape(padded, mine)
    own = [small_own[starts[i] : starts[i + 1]] for i in range(len(entries))]
    other = [small_other[starts[i] : starts[i + 1]] for i in range(len(entries))]
    conv_all = (
        by_seq(own[0].reshape(conv_rows, chips, piece), other[0].reshape(conv_rows, chips, piece))
        .transpose(1, 2, 0, 3)
        .reshape(conv_rows, filters)
        .astype(f32)
    )
    conv_bias_total = (
        by_seq(own[1].reshape(chips, piece), other[1].reshape(chips, piece))
        .transpose(1, 0, 2)
        .reshape(filters)
        .astype(f32)
    )
    highway_bias_total = (
        by_seq(own[2].reshape(2, chips, piece), other[2].reshape(2, chips, piece))
        .transpose(1, 2, 0, 3)
        .reshape(2 * filters)
        .astype(f32)
    )
    table_total = (own[3].astype(f32) + other[3].astype(f32)).reshape(-1)
    table_total = table_total[: vocab * features].reshape(vocab, features)
    norms = (own[4].astype(f32) + other[4].astype(f32)).reshape(4, model)
    position_total = small[:, 2 * share :].reshape(2 * words, model).astype(f32)
    kernel_grads = []
    first = 0
    for kernel in kernels:
        kernel_grads.append(conv_all[: kernel.shape[0], first : first + kernel.shape[1]])
        first = first + kernel.shape[1]
    return (
        layer_out[None],
        table_total,
        *kernel_grads,
        conv_bias_total,
        highway_total,
        highway_bias_total,
        projection_total,
        position_total,
        attention_total,
        output_total,
        norms[0],
        norms[1],
        inward_total,
        outward_total,
        norms[2],
        norms[3],
    )


def solution(mesh):
    placed = (
        P("dp", "seq", None),
        P("dp", "seq"),
        P("dp"),
        P(),
        P(),
        P(),
        P(),
        P(),
        P(),
        P(),
        P(),
        P(),
        P("dp", None),
        P(),
        P("dp", None),
        P(),
        P("dp", None),
        P("dp", None),
        P(),
        P(),
        P("dp", None),
        P("dp", None),
        P(),
        P(),
        P("dp", "seq", None),
    )
    return jax.shard_map(
        body,
        mesh=mesh,
        in_specs=placed,
        out_specs=(
            P("dp", "seq", None),
            P(),
            P(),
            P(),
            P(),
            P(),
            P(),
            P(),
            P(),
            P(),
            P("dp", None),
            P(),
            P("dp", None),
            P(),
            P("dp", None),
            P("dp", None),
            P(),
            P(),
            P("dp", None),
            P("dp", None),
            P(),
            P(),
        ),
        check_vma=False,
    )
```

```python
from functools import partial
import math

import jax
import jax.numpy as jnp
from jax import lax
from jax.experimental import pallas as pl
from jax.experimental.pallas import tpu as pltpu
from jax.sharding import PartitionSpec as P

HEAD_DIM = 64


exact_gelu = partial(jax.nn.gelu, approximate=False)


def layer_norm(value, gain, bias):
    mean = jnp.mean(value, axis=-1, keepdims=True)
    centered = value - mean
    spread = jnp.mean(centered * centered, axis=-1, keepdims=True)
    return centered * lax.rsqrt(spread + 1e-12) * gain + bias


def highway_mix(transform, gate, hidden):
    carry = jax.nn.sigmoid(gate)
    return carry * hidden + (1.0 - carry) * jax.nn.relu(transform)


def place():
    spot = lax.axis_index("dp")
    return (spot // 4, (spot // 2) % 2, spot % 2)


def core_swap(value):
    size = lax.axis_size("dp")
    return lax.ppermute(value, "dp", [(spot, spot ^ 1) for spot in range(size)])


def middle_swap(value):
    size = lax.axis_size("dp")
    return lax.ppermute(value, "dp", [(spot, spot ^ 2) for spot in range(size)])


def outer_shift(value, steps):
    size = lax.axis_size("dp")
    return lax.ppermute(value, "dp", [(spot, (spot - 4 * steps) % size) for spot in range(size)])


def seq_swap(value):
    return lax.ppermute(value, "seq", [(0, 1), (1, 0)])


def after(value, *others):
    return lax.optimization_barrier((value,) + others)[0]


def pick(value, index, axis):
    return lax.dynamic_index_in_dim(value, index, axis, keepdims=False)


def outer_pieces(shard):
    return [shard] + [outer_shift(shard, steps) for steps in range(1, lax.axis_size("dp") // 4)]


def gather_near(pieces):
    outer = place()[0]
    size = len(pieces)
    near = jnp.zeros((size,) + pieces[0].shape, pieces[0].dtype)
    for steps, piece in enumerate(pieces):
        near = lax.dynamic_update_index_in_dim(near, piece, (outer + steps) % size, 0)
    return near


def gather(values, side=None):
    _, middle, core = place()
    size = values[0].shape[0]
    shape = values[0].shape[1:]
    zeros = (0,) * len(shape)
    whole = jnp.zeros(((size, 2, 2) if side is None else (2, size, 2)) + shape, values[0].dtype)
    for flip, value in enumerate(values):
        flip_middle, flip_core = flip % 2, flip // 2
        if side is None:
            start = (0, middle ^ flip_middle, core ^ flip_core) + zeros
            value = value[:, None, None]
        else:
            start = (core ^ side ^ flip_core, 0, middle ^ flip_middle) + zeros
            value = value[None, :, None]
        whole = lax.dynamic_update_slice(whole, value, start)
    return whole


def scatter_core(parts, side=None):
    _, _, core = place()
    axis, slot = (2, core) if side is None else (0, core ^ side)
    other = core_swap(pick(parts, 1 - slot, axis).astype(jnp.bfloat16))
    return pick(parts, slot, axis).astype(jnp.float32) + other.astype(jnp.float32)


def scatter_middle(half, first=(), last=()):
    _, middle, _ = place()
    sent = after(pick(half, 1 - middle, 1).astype(jnp.bfloat16), *first)
    return pick(half, middle, 1) + after(middle_swap(sent), *last).astype(jnp.float32)


def scatter_outer(quarter, first=(), last=()):
    outer, _, _ = place()
    size = quarter.shape[0]
    rounded = after(quarter.astype(jnp.bfloat16), *first)
    pieces = [
        outer_shift(pick(rounded, (outer + size - steps) % size, 0), steps) for steps in range(1, size)
    ]
    if last:
        pieces = lax.optimization_barrier(tuple(pieces) + tuple(last))[: size - 1]
    total = pick(quarter, outer, 0)
    for value in pieces:
        total = total + value.astype(jnp.float32)
    return total


def seq_sum(value):
    return value + seq_swap(value.astype(jnp.bfloat16)).astype(jnp.float32)


def own_blocks(value, axis):
    axis = axis % value.ndim
    size = lax.axis_size("dp")
    shape = value.shape
    split = shape[:axis] + (size // 2, 2, shape[axis] // size) + shape[axis + 1 :]
    chosen = pick(value.reshape(split), lax.axis_index("seq"), axis + 1)
    return chosen.reshape(shape[:axis] + (shape[axis] // 2,) + shape[axis + 1 :])


def interleave(own, other, piece):
    first = lax.axis_index("seq") == 0
    blocks = []
    for start in range(0, own.shape[1], piece):
        mine, theirs = own[:, start : start + piece], other[:, start : start + piece]
        blocks += [jnp.where(first, mine, theirs), jnp.where(first, theirs, mine)]
    return jnp.concatenate(blocks, axis=1)


def halves_of(value, piece):
    first = lax.axis_index("seq") == 0
    own, other = [], []
    for start in range(0, value.shape[1], 2 * piece):
        even, odd = value[:, start : start + piece], value[:, start + piece : start + 2 * piece]
        own.append(jnp.where(first, even, odd))
        other.append(jnp.where(first, odd, even))
    return jnp.concatenate(own, axis=1), jnp.concatenate(other, axis=1)


def by_seq(own, other):
    first = lax.axis_index("seq") == 0
    return jnp.stack([jnp.where(first, own, other), jnp.where(first, other, own)])


WIDTHS = 7
LANES = 128
NEG = -1e30


def conv_forward_kernel(spread_ref, lens_ref, weight_ref, pooled_ref, ties_ref, window_ref, flipped_ref, scores_ref):
    letters, words, _ = spread_ref.shape
    channels = weight_ref.shape[1]
    lane = lax.broadcasted_iota(jnp.int32, (words, LANES), 1)
    slot = lane // 16
    limit = jnp.maximum(lens_ref[...] - (lane - 16 * WIDTHS), 1)
    for p in range(letters):
        window = jnp.zeros((words, LANES), jnp.float32)
        for j in range(WIDTHS):
            if p + j < letters:
                window = jnp.where(slot == j, spread_ref[p + j].astype(jnp.float32), window)
        flag = jnp.where((lane >= 16 * WIDTHS) & (lane < 17 * WIDTHS) & (p >= limit), 1.0, window)
        window_ref[p * words:(p + 1) * words] = flag.astype(jnp.bfloat16)
    flipped_ref[...] = window_ref[...].T
    tile = 256

    def one_tile(index, _):
        c = pl.multiple_of(index * tile, tile)
        scores_ref[...] = jnp.dot(window_ref[...], weight_ref[:, pl.ds(c, tile)], preferred_element_type=jnp.float32)
        for r in range(0, words, 16):
            top = scores_ref[r:r + 16]
            for p in range(1, letters):
                top = jnp.maximum(top, scores_ref[p * words + r:p * words + r + 16])
            count = jnp.zeros((16, tile), jnp.float32)
            for p in range(letters):
                count += jnp.where(scores_ref[p * words + r:p * words + r + 16] == top, 1.0, 0.0)
            pooled_ref[r:r + 16, pl.ds(c, tile)] = top
            ties_ref[r:r + 16, pl.ds(c, tile)] = count
        return 0

    lax.fori_loop(0, channels // tile, one_tile, 0)


def conv_backward_kernel(window_ref, flipped_ref, codes_ref, weight_ref, turned_ref, pooled_ref, share_in_ref,
                         grad_ref, table_ref, share_ref, scores_ref, spread_ref, letters):
    rows = window_ref.shape[0]
    words = rows // letters
    channels = weight_ref.shape[1]
    vocab = table_ref.shape[0]
    tile = 256

    @pl.when(pl.program_id(0) == 0)
    def _():
        grad_ref[...] = jnp.zeros_like(grad_ref)
        table_ref[...] = jnp.zeros_like(table_ref)

    def one_tile(index, _):
        c = pl.multiple_of(index * tile, tile)
        scores_ref[...] = jnp.dot(window_ref[...], weight_ref[:, pl.ds(c, tile)], preferred_element_type=jnp.float32)
        for r in range(0, words, 16):
            top = pooled_ref[r:r + 16, pl.ds(c, tile)]
            part = share_in_ref[r:r + 16, pl.ds(c, tile)]
            for p in range(letters):
                hit = scores_ref[p * words + r:p * words + r + 16] == top
                share_ref[p * words + r:p * words + r + 16, pl.ds(c, tile)] = jnp.where(hit, part, 0.0).astype(jnp.bfloat16)
        return 0

    lax.fori_loop(0, channels // tile, one_tile, 0)
    grad_ref[...] += jnp.dot(flipped_ref[...], share_ref[...], preferred_element_type=jnp.float32)
    scores_ref[:, :LANES] = jnp.dot(share_ref[...], turned_ref[...], preferred_element_type=jnp.float32)
    slot = lax.broadcasted_iota(jnp.int32, (words, LANES), 1) // 16
    for c in range(letters):
        spread = jnp.zeros((words, LANES), jnp.float32)
        for j in range(WIDTHS):
            if c - j >= 0:
                spread = jnp.where(slot == j, scores_ref[(c - j) * words:(c - j + 1) * words, :LANES], spread)
        spread_ref[c * words:(c + 1) * words] = spread.astype(jnp.bfloat16)
    onehot = jnp.where(lax.broadcasted_iota(jnp.int32, (vocab, rows), 0) == codes_ref[0], 1.0, 0.0).astype(jnp.bfloat16)
    table_ref[...] += jnp.dot(onehot, spread_ref[...], preferred_element_type=jnp.float32)


def conv_forward(spread, lens, weight, block):
    letters, words, _ = spread.shape
    channels = weight.shape[1]
    steps = words // block
    rows = letters * block
    f32 = jnp.float32
    return pl.pallas_call(
        conv_forward_kernel,
        grid=(steps,),
        in_specs=[
            pl.BlockSpec((letters, block, LANES), lambda i: (0, i, 0)),
            pl.BlockSpec((block, 1), lambda i: (i, 0)),
            pl.BlockSpec((LANES, channels), lambda i: (0, 0)),
        ],
        out_specs=[
            pl.BlockSpec((block, channels), lambda i: (i, 0)),
            pl.BlockSpec((block, channels), lambda i: (i, 0)),
            pl.BlockSpec((rows, LANES), lambda i: (i, 0)),
            pl.BlockSpec((LANES, rows), lambda i: (0, i)),
        ],
        out_shape=[
            jax.ShapeDtypeStruct((words, channels), f32),
            jax.ShapeDtypeStruct((words, channels), f32),
            jax.ShapeDtypeStruct((steps * rows, LANES), jnp.bfloat16),
            jax.ShapeDtypeStruct((LANES, steps * rows), jnp.bfloat16),
        ],
        scratch_shapes=[pltpu.VMEM((rows, 256), f32)],
        compiler_params=pltpu.CompilerParams(dimension_semantics=("arbitrary",)),
        cost_estimate=pl.CostEstimate(
            flops=2 * LANES * steps * rows * channels,
            bytes_accessed=steps * rows * channels * 5,
            transcendentals=0,
        ),
        name="conv_forward",
    )(spread, lens, weight)


def conv_backward(window, flipped, codes, weight, turned, pooled, share, vocab, block, first, steps):
    words, channels = pooled.shape
    rows = window.shape[0] // (words // block)
    letters = rows // block
    f32 = jnp.float32
    vocab = -(-vocab // 16) * 16

    def kernel(*refs):
        conv_backward_kernel(*refs, letters=letters)

    return pl.pallas_call(
        kernel,
        grid=(steps,),
        in_specs=[
            pl.BlockSpec((rows, LANES), lambda i: (first + i, 0)),
            pl.BlockSpec((LANES, rows), lambda i: (0, first + i)),
            pl.BlockSpec((1, 1, rows), lambda i: (first + i, 0, 0)),
            pl.BlockSpec((LANES, channels), lambda i: (0, 0)),
            pl.BlockSpec((channels, LANES), lambda i: (0, 0)),
            pl.BlockSpec((block, channels), lambda i: (first + i, 0)),
            pl.BlockSpec((block, channels), lambda i: (first + i, 0)),
        ],
        out_specs=[
            pl.BlockSpec((LANES, channels), lambda i: (0, 0)),
            pl.BlockSpec((vocab, LANES), lambda i: (0, 0)),
        ],
        out_shape=[
            jax.ShapeDtypeStruct((LANES, channels), f32),
            jax.ShapeDtypeStruct((vocab, LANES), f32),
        ],
        scratch_shapes=[
            pltpu.VMEM((rows, channels), jnp.bfloat16),
            pltpu.VMEM((rows, 256), f32),
            pltpu.VMEM((rows, LANES), jnp.bfloat16),
        ],
        compiler_params=pltpu.CompilerParams(dimension_semantics=("arbitrary",)),
        cost_estimate=pl.CostEstimate(
            flops=6 * LANES * steps * rows * channels,
            bytes_accessed=steps * rows * channels * 8,
            transcendentals=0,
        ),
        name="conv_backward",
    )(window, flipped, codes, weight, turned, pooled, share)


def merge_kernel(*refs):
    whole_ref = refs[-1]
    whole_ref[...] = jnp.zeros_like(whole_ref)
    features = refs[0].shape[0]
    first = 0
    for width, kernel_ref in enumerate(refs[:-1], 1):
        channels = kernel_ref.shape[1]
        whole_ref[: width * features, first : first + channels] = kernel_ref[...]
        marks = lax.broadcasted_iota(jnp.int32, (16, channels), 0) == width - 1
        whole_ref[WIDTHS * features :, first : first + channels] = jnp.where(marks, NEG, 0.0).astype(jnp.bfloat16)
        first = first + channels


def merged_weight(kernels):
    channels = sum(kernel.shape[1] for kernel in kernels)
    return pl.pallas_call(
        merge_kernel, out_shape=jax.ShapeDtypeStruct((LANES, channels), jnp.bfloat16), name="merge_widths"
    )(*kernels)


def spread_letters(codes, table):
    vocab, features = table.shape
    words, letters = codes.shape
    wide = jnp.tile(table, (1, LANES // features))
    onehot = (codes.T.reshape(-1, 1) == jnp.arange(vocab, dtype=jnp.int32)[None, :]).astype(jnp.bfloat16)
    return jnp.dot(onehot, wide, preferred_element_type=jnp.float32).astype(jnp.bfloat16).reshape(letters, words, LANES)


def score_heads(query_heads, key_heads, keep):
    raw = (
        jnp.einsum("qhd,khd->hqk", query_heads, key_heads, preferred_element_type=jnp.float32)
        * 0.125
    )
    return jnp.where(keep[None, None, :], raw, -1e30)


def body(
    character_codes,
    word_lengths,
    sequence_lengths,
    character_table,
    conv_width1,
    conv_width2,
    conv_width3,
    conv_width4,
    conv_width5,
    conv_width6,
    conv_width7,
    conv_bias,
    highway_weight,
    highway_bias,
    projection,
    position_table,
    attention_in,
    attention_out,
    norm1_gain,
    norm1_bias,
    hidden_in,
    hidden_out,
    norm2_gain,
    norm2_bias,
    cotangent,
):
    kernels = (
        conv_width1,
        conv_width2,
        conv_width3,
        conv_width4,
        conv_width5,
        conv_width6,
        conv_width7,
    )
    f32 = jnp.float32
    low = jnp.bfloat16
    side = lax.axis_index("seq")
    outer, middle, core = place()
    size = lax.axis_size("dp")
    chips = size // 2
    words = character_codes.shape[1]
    letters = character_codes.shape[2]
    vocab, features = character_table.shape
    filters = conv_bias.shape[0]
    mine = filters // 2
    piece = filters // size
    half = piece // 2
    model = position_table.shape[1]
    block = math.gcd(words, 64)
    steps = words // block

    highway_shard = own_blocks(highway_weight.reshape(-1, 2, filters), 2)
    held = lax.dynamic_slice_in_dim(projection, core * half, half, 0)
    lent = lax.dynamic_slice_in_dim(projection, (1 - core) * half, half, 0)
    projection_shard = jnp.where(core == side, held, core_swap(lent))
    code_rows = jnp.concatenate([character_codes[0], word_lengths[0][:, None]], axis=1)
    code_rows = [code_rows, seq_swap(code_rows)]

    highway_all = lax.all_gather(highway_shard.reshape(piece, filters), "dp", axis=0, tiled=True)
    highway_parts = [highway_all[:, :mine], highway_all[:, mine:]]
    projection_near = gather_near(outer_pieces(projection_shard))
    projection_across = middle_swap(projection_near)
    projection_far = [core_swap(projection_near), core_swap(projection_across)]
    projection_full = gather((projection_near, projection_across, *projection_far)).reshape(mine, model)
    attention_near = gather_near(
        outer_pieces(after(jnp.concatenate([attention_in, attention_out], axis=1), projection_near))
    )
    def cut(grad, slots=False):
        lead = (2, size // 4, 2) if slots else (size // 4, 2, 2)
        return grad.reshape(lead + (grad.shape[0] // size,) + grad.shape[1:])

    code_rows[1] = after(code_rows[1], projection_near)
    codes = [rows[:, :letters] for rows in code_rows]
    conv_weight = own_blocks(merged_weight(kernels), 1)
    conv_shift = own_blocks(conv_bias, 0).astype(f32)
    forwards = [
        conv_forward(spread_letters(codes[0], character_table), code_rows[0][:, letters:], conv_weight, block)
    ]
    rows = hidden_in.shape[0]
    splits = hidden_out.shape[0] // rows
    inner_size = hidden_in.shape[1]
    turned_in = hidden_in.reshape(rows, size, splits, rows).transpose(0, 2, 1, 3).reshape(rows, inner_size)
    forward_shard = jnp.concatenate(
        [turned_in] + [hidden_out[part * rows : (part + 1) * rows] for part in range(splits)], axis=1
    )
    forward_all = lax.all_gather(after(forward_shard, forwards[0][0]), "dp", axis=0, tiled=True)
    inward_full = forward_all[:, :inner_size]
    outward_parts = [
        forward_all[:, inner_size + part * model : inner_size + (part + 1) * model] for part in range(splits)
    ]
    forwards.append(
        conv_forward(spread_letters(codes[1], character_table), code_rows[1][:, letters:], conv_weight, block)
    )
    biased = [forward[0] + conv_shift for forward in forwards]
    hidden0_parts = [jax.nn.relu(value) for value in biased]
    hidden0_low = [value.astype(low) for value in hidden0_parts]
    swapped = [seq_swap(value) for value in hidden0_low]
    hidden0_all = jnp.concatenate(
        [interleave(hidden0_low[0], swapped[1], piece), interleave(hidden0_low[1], swapped[0], piece)], axis=0
    )
    hidden0 = jnp.concatenate(hidden0_parts, axis=0)
    highway_shift = own_blocks(highway_bias.reshape(2, filters), 1).astype(f32)
    transform, gate = [
        jnp.dot(hidden0_all, highway_parts[part], preferred_element_type=f32) + highway_shift[part]
        for part in range(2)
    ]
    hidden1 = highway_mix(transform, gate, hidden0)
    hidden1_low = hidden1.astype(low)
    attention_across = after(middle_swap(attention_near), hidden1_low)
    attention_far = [core_swap(attention_near), core_swap(attention_across)]
    attention_all = gather((attention_near, attention_across, *attention_far)).reshape(model, -1)
    attention_full = attention_all[:, : 3 * model]
    output_full = attention_all[:, 3 * model :]
    mapped = jnp.dot(hidden1_low, projection_full, preferred_element_type=f32)
    offset = side * words
    positions = lax.dynamic_slice_in_dim(position_table, offset, words, 0).astype(f32)
    embedded = mapped[:words] + seq_swap(mapped[words:].astype(low)).astype(f32) + positions
    embedded_low = embedded.astype(low)
    heads = model // HEAD_DIM
    projected = jnp.dot(embedded_low, attention_full, preferred_element_type=f32).astype(low)
    gathered = jnp.concatenate(
        [
            jnp.concatenate([pair, seq_swap(pair)], axis=0)
            for pair in (projected[:, model : 2 * model], projected[:, 2 * model :])
        ],
        axis=1,
    )
    length = gathered.shape[0]
    query_heads = projected[:, :model].reshape(words, heads, HEAD_DIM)
    key_heads = gathered[:, :model].reshape(length, heads, HEAD_DIM)
    value_heads = gathered[:, model:].reshape(length, heads, HEAD_DIM)
    keep = (jnp.arange(length, dtype=jnp.int32) + offset) % length < sequence_lengths[0]
    scores = score_heads(query_heads, key_heads, keep)
    top = jnp.max(scores, axis=-1, keepdims=True)
    unnormalized = jnp.exp(scores - top)
    total = jnp.sum(unnormalized, axis=-1, keepdims=True)
    probs_low = (unnormalized / total).astype(jnp.bfloat16)
    attended = jnp.einsum(
        "hqk,khd->qhd", probs_low, value_heads, preferred_element_type=jnp.float32
    )
    attended = attended.reshape(words, model).astype(jnp.bfloat16)
    joined = embedded + jnp.dot(attended, output_full, preferred_element_type=jnp.float32)
    gain1 = norm1_gain.astype(jnp.float32)
    shift1 = norm1_bias.astype(jnp.float32)
    gain2 = norm2_gain.astype(jnp.float32)
    shift2 = norm2_bias.astype(jnp.float32)
    normed1 = layer_norm(joined, gain1, shift1)
    normed1_low = normed1.astype(jnp.bfloat16)
    inner = jnp.dot(normed1_low, inward_full, preferred_element_type=jnp.float32)
    active = exact_gelu(inner).astype(jnp.bfloat16)
    actives = [active[:, part * model : (part + 1) * model] for part in range(splits)]
    summed = normed1 + sum(
        jnp.dot(actives[part], outward_parts[part], preferred_element_type=f32) for part in range(splits)
    )
    layer_out = layer_norm(summed, gain2, shift2).astype(jnp.bfloat16)
    seed_grad = cotangent[0].astype(jnp.float32)
    _, norm2_pull = jax.vjp(layer_norm, summed, gain2, shift2)
    grad_summed, norm2_gain_grad, norm2_bias_grad = norm2_pull(seed_grad)
    grad_outer = grad_summed.astype(jnp.bfloat16)
    hidden_out_grads = [
        jnp.einsum("tf,td->fd", part, grad_outer, preferred_element_type=f32).astype(low) for part in actives
    ]
    grad_active = jnp.concatenate(
        [jnp.einsum("td,fd->tf", grad_outer, part, preferred_element_type=f32) for part in outward_parts], axis=1
    )
    _, gelu_pull = jax.vjp(exact_gelu, inner)
    grad_inner = gelu_pull(grad_active)[0].astype(jnp.bfloat16)
    hidden_in_grad = jnp.einsum(
        "td,tf->df", normed1_low, grad_inner, preferred_element_type=jnp.float32
    ).astype(low)
    grad_normed1 = grad_summed + jnp.einsum(
        "tf,df->td", grad_inner, inward_full, preferred_element_type=jnp.float32
    )
    _, norm1_pull = jax.vjp(layer_norm, joined, gain1, shift1)
    grad_joined, norm1_gain_grad, norm1_bias_grad = norm1_pull(grad_normed1)
    forward_grad = jnp.concatenate([hidden_in_grad] + hidden_out_grads, axis=1)
    forward_sum = lax.psum_scatter(forward_grad, "dp", scatter_dimension=0, tiled=True)
    grad_branch = after(grad_joined.astype(low), forward_grad)
    attention_out_grad = jnp.einsum(
        "td,te->de", attended, grad_branch, preferred_element_type=jnp.float32
    ).astype(low)
    grad_attended = jnp.einsum(
        "te,de->td", grad_branch, output_full, preferred_element_type=jnp.float32
    ).astype(jnp.bfloat16)
    grad_heads = grad_attended.reshape(words, heads, HEAD_DIM)
    probs = jnp.exp(score_heads(query_heads, key_heads, keep) - top) / total
    probs_again = probs.astype(jnp.bfloat16)
    value_grad = jnp.einsum("hqk,qhd->khd", probs_again, grad_heads, preferred_element_type=f32)
    grad_probs = jnp.einsum(
        "qhd,khd->hqk", grad_heads, value_heads, preferred_element_type=jnp.float32
    )
    grad_scores = (
        probs * (grad_probs - jnp.sum(probs * grad_probs, axis=-1, keepdims=True))
    ).astype(jnp.bfloat16)
    grad_query = (
        jnp.einsum("hqk,khd->qhd", grad_scores, key_heads, preferred_element_type=jnp.float32)
        * 0.125
    )
    key_grad = (
        jnp.einsum("hqk,qhd->khd", grad_scores, query_heads, preferred_element_type=f32) * 0.125
    )
    value_grad = value_grad.reshape(length, model)
    key_grad = key_grad.reshape(length, model)
    value_back = seq_swap(value_grad[words:].astype(low))
    key_back = seq_swap(key_grad[words:].astype(low))
    grad_pairs = jnp.concatenate(
        [key_grad[:words] + key_back.astype(f32), value_grad[:words] + value_back.astype(f32)], axis=1
    )
    grad_projected = jnp.concatenate([grad_query.reshape(words, model), grad_pairs], axis=1).astype(low)
    attention_in_grad = jnp.einsum(
        "td,te->de", embedded_low, grad_projected, preferred_element_type=f32
    ).astype(low)
    grad_embedded = grad_joined + jnp.einsum(
        "te,de->td", grad_projected, attention_full, preferred_element_type=f32
    )
    grad_mapped = grad_embedded.astype(low)
    attention_half = scatter_core(cut(jnp.concatenate([attention_in_grad, attention_out_grad], axis=1)))
    grad_mapped = jnp.concatenate([grad_mapped, seq_swap(grad_mapped)], axis=0)
    grad_mapped = after(grad_mapped, attention_half)
    projection_grad = jnp.einsum(
        "tf,td->fd", hidden1_low, grad_mapped, preferred_element_type=f32
    ).astype(low)
    grad_hidden1 = jnp.einsum("td,fd->tf", grad_mapped, projection_full, preferred_element_type=f32)
    _, highway_pull = jax.vjp(highway_mix, transform, gate, hidden0)
    grad_transform, grad_gate, grad_carry = highway_pull(grad_hidden1)
    grad_gates = [grad_transform.astype(low), grad_gate.astype(low)]
    grad_spread = sum(
        jnp.einsum("tg,fg->tf", grad_gates[part], highway_parts[part], preferred_element_type=f32)
        for part in range(2)
    )
    grad_held, grad_lent = halves_of(grad_spread, piece)
    grad_lent = grad_lent.astype(low)
    lent_back = [seq_swap(grad_lent[words:]), seq_swap(grad_lent[:words])]
    highway_grads = [
        jnp.einsum("tf,tg->fg", hidden0_all, grad_gates[part], preferred_element_type=f32).astype(low)
        for part in range(2)
    ]
    joint_half = scatter_core(
        cut(jnp.concatenate([highway_grads[1], projection_grad.reshape(filters, model // 2)], axis=1))
    )
    attention_quarter = scatter_middle(attention_half)
    lent_back[1] = after(lent_back[1], joint_half, attention_quarter)
    grad_near = grad_carry + grad_held
    grad_pooled = [
        jnp.where(
            biased[part] > 0, grad_near[part * words : (part + 1) * words] + lent_back[part].astype(f32), 0.0
        )
        for part in range(2)
    ]
    highway_bias_grad = jnp.concatenate([jnp.sum(grad.astype(f32), axis=0) for grad in grad_gates])
    conv_bias_grad = jnp.sum(grad_pooled[0], axis=0) + jnp.sum(grad_pooled[1], axis=0)
    position_rows = 2 * words * model // mine // size
    position_low = grad_embedded.astype(low)
    nothing = jnp.zeros_like(position_low)
    position_grad = by_seq(position_low, nothing).reshape(size, position_rows, mine)
    highway_rows = jnp.concatenate(
        [highway_grads[0].reshape(size, piece, mine), position_grad], axis=1
    ).reshape(-1, mine)
    highway_sum = lax.psum_scatter(
        after(highway_rows, forward_sum), "dp", scatter_dimension=0, tiled=True
    )
    turned = conv_weight.T
    shares = [grad_pooled[part] / forwards[part][1] for part in range(2)]
    code_blocks = [
        codes[part].reshape(steps, block, letters).transpose(0, 2, 1).reshape(steps, 1, letters * block)
        for part in range(2)
    ]

    def back(part, first, count, *others):
        return conv_backward(
            forwards[part][2],
            forwards[part][3],
            code_blocks[part],
            conv_weight,
            turned,
            forwards[part][0],
            after(shares[part], *others),
            vocab,
            block,
            first,
            count,
        )

    cuts = steps // 2
    backs = [back(0, 0, cuts, attention_quarter, joint_half, highway_rows)]
    attention_sum = scatter_outer(attention_quarter, grad_pooled, backs[0])
    joint_quarter = scatter_middle(joint_half, (), backs[0])
    backs.append(back(0, cuts, steps - cuts, attention_sum, joint_quarter, *backs[0]))
    forward_both = forward_sum.astype(f32) + after(seq_swap(after(forward_sum, *backs[0])), *backs[1]).astype(f32)
    backs.append(back(1, 0, cuts, forward_sum, *backs[1]))
    attention_both = attention_sum + after(seq_swap(after(attention_sum.astype(low), *backs[1])), *backs[2]).astype(f32)
    backs.append(back(1, cuts, steps - cuts, forward_both, *backs[2]))
    joint_sum = scatter_outer(joint_quarter, backs[0], backs[3])
    merged_grad = backs[0][0] + backs[1][0] + backs[2][0] + backs[3][0]
    table_wide = backs[0][1] + backs[1][1] + backs[2][1] + backs[3][1]
    table_grad = sum(
        table_wide[:vocab, shift * features : (shift + 1) * features] for shift in range(WIDTHS)
    )

    forward_total = forward_both
    inward_total = (
        forward_total[:, :inner_size].reshape(rows, splits, size, rows).transpose(0, 2, 1, 3).reshape(rows, inner_size)
    )
    outward_total = jnp.concatenate(
        [forward_total[:, inner_size + part * model : inner_size + (part + 1) * model] for part in range(splits)],
        axis=0,
    )
    attention_total = attention_both[:, : 3 * model]
    output_total = attention_both[:, 3 * model :]
    part0 = highway_sum[:piece]
    position_part = highway_sum[piece:]
    position_part = (position_part.astype(f32) + seq_swap(position_part).astype(f32)).astype(low)
    part1 = joint_sum.astype(low)
    projection_part = part1[:, mine:].reshape(half, model)
    projection_pair = core_swap(projection_part)
    projection_sum = jnp.concatenate(
        [
            jnp.where(core == 0, projection_part, projection_pair),
            jnp.where(core == 0, projection_pair, projection_part),
        ],
        axis=0,
    )
    finals = jnp.concatenate([part0, part1[:, :mine], projection_sum], axis=1)
    finals_other = seq_swap(finals)
    projection_total = jnp.where(core == side, finals[:, 2 * mine :], finals_other[:, 2 * mine :]).astype(f32)
    highway_total = (
        by_seq(
            finals[:, : 2 * mine].reshape(piece, 2, chips, piece),
            finals_other[:, : 2 * mine].reshape(piece, 2, chips, piece),
        )
        .transpose(1, 2, 3, 0, 4)
        .reshape(piece, 2 * filters)
        .astype(f32)
    )

    conv_rows = WIDTHS * features
    table_rows = -(-vocab * features // mine)
    table_flat = jnp.pad(table_grad.reshape(-1), (0, table_rows * mine - vocab * features))
    entries = [
        merged_grad[:conv_rows],
        conv_bias_grad[None],
        highway_bias_grad.reshape(2, mine),
        table_flat.reshape(table_rows, mine),
        jnp.concatenate([norm1_gain_grad, norm1_bias_grad, norm2_gain_grad, norm2_bias_grad]).reshape(-1, mine),
    ]
    starts = [0]
    for row in entries:
        starts.append(starts[-1] + row.shape[0])
    padded = -(-starts[-1] // size) * size
    small = jnp.pad(jnp.concatenate(entries, axis=0), ((0, padded - starts[-1]), (0, 0)))
    small = after(small, joint_sum, attention_both, highway_sum)
    small = scatter_outer(scatter_middle(scatter_core(cut(small)))).astype(low)
    share = small.shape[0]
    small = after(jnp.concatenate([small, seq_swap(small), position_part], axis=0), finals_other)
    near = gather_near(outer_pieces(small))
    across = middle_swap(near)
    small = gather((near, across, core_swap(near), core_swap(across))).reshape(size, -1, mine)
    small_own = small[:, :share].reshape(padded, mine)
    small_other = small[:, share : 2 * share].reshape(padded, mine)
    own = [small_own[starts[i] : starts[i + 1]] for i in range(len(entries))]
    other = [small_other[starts[i] : starts[i + 1]] for i in range(len(entries))]
    conv_all = (
        by_seq(own[0].reshape(conv_rows, chips, piece), other[0].reshape(conv_rows, chips, piece))
        .transpose(1, 2, 0, 3)
        .reshape(conv_rows, filters)
        .astype(f32)
    )
    conv_bias_total = (
        by_seq(own[1].reshape(chips, piece), other[1].reshape(chips, piece))
        .transpose(1, 0, 2)
        .reshape(filters)
        .astype(f32)
    )
    highway_bias_total = (
        by_seq(own[2].reshape(2, chips, piece), other[2].reshape(2, chips, piece))
        .transpose(1, 2, 0, 3)
        .reshape(2 * filters)
        .astype(f32)
    )
    table_total = (own[3].astype(f32) + other[3].astype(f32)).reshape(-1)
    table_total = table_total[: vocab * features].reshape(vocab, features)
    norms = (own[4].astype(f32) + other[4].astype(f32)).reshape(4, model)
    position_total = small[:, 2 * share :].reshape(2 * words, model).astype(f32)
    kernel_grads = []
    first = 0
    for kernel in kernels:
        kernel_grads.append(conv_all[: kernel.shape[0], first : first + kernel.shape[1]])
        first = first + kernel.shape[1]
    return (
        layer_out[None],
        table_total,
        *kernel_grads,
        conv_bias_total,
        highway_total,
        highway_bias_total,
        projection_total,
        position_total,
        attention_total,
        output_total,
        norms[0],
        norms[1],
        inward_total,
        outward_total,
        norms[2],
        norms[3],
    )


def solution(mesh):
    placed = (
        P("dp", "seq", None),
        P("dp", "seq"),
        P("dp"),
        P(),
        P(),
        P(),
        P(),
        P(),
        P(),
        P(),
        P(),
        P(),
        P("dp", None),
        P(),
        P("dp", None),
        P(),
        P("dp", None),
        P("dp", None),
        P(),
        P(),
        P("dp", None),
        P("dp", None),
        P(),
        P(),
        P("dp", "seq", None),
    )
    return jax.shard_map(
        body,
        mesh=mesh,
        in_specs=placed,
        out_specs=(
            P("dp", "seq", None),
            P(),
            P(),
            P(),
            P(),
            P(),
            P(),
            P(),
            P(),
            P(),
            P("dp", None),
            P(),
            P("dp", None),
            P(),
            P("dp", None),
            P("dp", None),
            P(),
            P(),
            P("dp", None),
            P("dp", None),
            P(),
            P(),
        ),
        check_vma=False,
    )
```

```python
from functools import partial
import math

import jax
import jax.numpy as jnp
from jax import lax
from jax.experimental import pallas as pl
from jax.experimental.pallas import tpu as pltpu
from jax.sharding import PartitionSpec as P

HEAD_DIM = 64


exact_gelu = partial(jax.nn.gelu, approximate=False)


def layer_norm(value, gain, bias):
    mean = jnp.mean(value, axis=-1, keepdims=True)
    centered = value - mean
    spread = jnp.mean(centered * centered, axis=-1, keepdims=True)
    return centered * lax.rsqrt(spread + 1e-12) * gain + bias


def highway_mix(transform, gate, hidden):
    carry = jax.nn.sigmoid(gate)
    return carry * hidden + (1.0 - carry) * jax.nn.relu(transform)


def place():
    spot = lax.axis_index("dp")
    return (spot // 4, (spot // 2) % 2, spot % 2)


def core_swap(value):
    size = lax.axis_size("dp")
    return lax.ppermute(value, "dp", [(spot, spot ^ 1) for spot in range(size)])


def middle_swap(value):
    size = lax.axis_size("dp")
    return lax.ppermute(value, "dp", [(spot, spot ^ 2) for spot in range(size)])


def outer_shift(value, steps):
    size = lax.axis_size("dp")
    return lax.ppermute(value, "dp", [(spot, (spot - 4 * steps) % size) for spot in range(size)])


def seq_swap(value):
    return lax.ppermute(value, "seq", [(0, 1), (1, 0)])


def after(value, *others):
    return lax.optimization_barrier((value,) + others)[0]


def pick(value, index, axis):
    return lax.dynamic_index_in_dim(value, index, axis, keepdims=False)


def outer_pieces(shard):
    return [shard] + [outer_shift(shard, steps) for steps in range(1, lax.axis_size("dp") // 4)]


def gather_near(pieces):
    outer = place()[0]
    size = len(pieces)
    near = jnp.zeros((size,) + pieces[0].shape, pieces[0].dtype)
    for steps, piece in enumerate(pieces):
        near = lax.dynamic_update_index_in_dim(near, piece, (outer + steps) % size, 0)
    return near


def gather(values, side=None):
    _, middle, core = place()
    size = values[0].shape[0]
    shape = values[0].shape[1:]
    zeros = (0,) * len(shape)
    whole = jnp.zeros(((size, 2, 2) if side is None else (2, size, 2)) + shape, values[0].dtype)
    for flip, value in enumerate(values):
        flip_middle, flip_core = flip % 2, flip // 2
        if side is None:
            start = (0, middle ^ flip_middle, core ^ flip_core) + zeros
            value = value[:, None, None]
        else:
            start = (core ^ side ^ flip_core, 0, middle ^ flip_middle) + zeros
            value = value[None, :, None]
        whole = lax.dynamic_update_slice(whole, value, start)
    return whole


def scatter_core(parts, side=None):
    _, _, core = place()
    axis, slot = (2, core) if side is None else (0, core ^ side)
    other = core_swap(pick(parts, 1 - slot, axis).astype(jnp.bfloat16))
    return pick(parts, slot, axis).astype(jnp.float32) + other.astype(jnp.float32)


def scatter_middle(half, first=(), last=()):
    _, middle, _ = place()
    sent = after(pick(half, 1 - middle, 1).astype(jnp.bfloat16), *first)
    return pick(half, middle, 1) + after(middle_swap(sent), *last).astype(jnp.float32)


def scatter_outer(quarter, first=(), last=()):
    outer, _, _ = place()
    size = quarter.shape[0]
    rounded = after(quarter.astype(jnp.bfloat16), *first)
    pieces = [
        outer_shift(pick(rounded, (outer + size - steps) % size, 0), steps) for steps in range(1, size)
    ]
    if last:
        pieces = lax.optimization_barrier(tuple(pieces) + tuple(last))[: size - 1]
    total = pick(quarter, outer, 0)
    for value in pieces:
        total = total + value.astype(jnp.float32)
    return total


def seq_sum(value):
    return value + seq_swap(value.astype(jnp.bfloat16)).astype(jnp.float32)


def own_blocks(value, axis):
    axis = axis % value.ndim
    size = lax.axis_size("dp")
    shape = value.shape
    split = shape[:axis] + (size // 2, 2, shape[axis] // size) + shape[axis + 1 :]
    chosen = pick(value.reshape(split), lax.axis_index("seq"), axis + 1)
    return chosen.reshape(shape[:axis] + (shape[axis] // 2,) + shape[axis + 1 :])


def interleave(own, other, piece):
    first = lax.axis_index("seq") == 0
    blocks = []
    for start in range(0, own.shape[1], piece):
        mine, theirs = own[:, start : start + piece], other[:, start : start + piece]
        blocks += [jnp.where(first, mine, theirs), jnp.where(first, theirs, mine)]
    return jnp.concatenate(blocks, axis=1)


def halves_of(value, piece):
    first = lax.axis_index("seq") == 0
    own, other = [], []
    for start in range(0, value.shape[1], 2 * piece):
        even, odd = value[:, start : start + piece], value[:, start + piece : start + 2 * piece]
        own.append(jnp.where(first, even, odd))
        other.append(jnp.where(first, odd, even))
    return jnp.concatenate(own, axis=1), jnp.concatenate(other, axis=1)


def by_seq(own, other):
    first = lax.axis_index("seq") == 0
    return jnp.stack([jnp.where(first, own, other), jnp.where(first, other, own)])


WIDTHS = 7
LANES = 128
NEG = -1e30


def conv_forward_kernel(spread_ref, lens_ref, weight_ref, pooled_ref, ties_ref, window_ref, flipped_ref, scores_ref):
    letters, words, _ = spread_ref.shape
    channels = weight_ref.shape[1]
    lane = lax.broadcasted_iota(jnp.int32, (words, LANES), 1)
    slot = lane // 16
    limit = jnp.maximum(lens_ref[...] - (lane - 16 * WIDTHS), 1)
    for p in range(letters):
        window = jnp.zeros((words, LANES), jnp.float32)
        for j in range(WIDTHS):
            if p + j < letters:
                window = jnp.where(slot == j, spread_ref[p + j].astype(jnp.float32), window)
        flag = jnp.where((lane >= 16 * WIDTHS) & (lane < 17 * WIDTHS) & (p >= limit), 1.0, window)
        window_ref[p * words:(p + 1) * words] = flag.astype(jnp.bfloat16)
    flipped_ref[...] = window_ref[...].T
    tile = 256

    def one_tile(index, _):
        c = pl.multiple_of(index * tile, tile)
        scores_ref[...] = jnp.dot(window_ref[...], weight_ref[:, pl.ds(c, tile)], preferred_element_type=jnp.float32)
        for r in range(0, words, 16):
            top = scores_ref[r:r + 16]
            for p in range(1, letters):
                top = jnp.maximum(top, scores_ref[p * words + r:p * words + r + 16])
            count = jnp.zeros((16, tile), jnp.float32)
            for p in range(letters):
                count += jnp.where(scores_ref[p * words + r:p * words + r + 16] == top, 1.0, 0.0)
            pooled_ref[r:r + 16, pl.ds(c, tile)] = top
            ties_ref[r:r + 16, pl.ds(c, tile)] = count
        return 0

    lax.fori_loop(0, channels // tile, one_tile, 0)


def conv_backward_kernel(window_ref, flipped_ref, codes_ref, weight_ref, turned_ref, pooled_ref, share_in_ref,
                         grad_ref, table_ref, share_ref, scores_ref, spread_ref, letters, narrow):
    rows = window_ref.shape[0]
    words = rows // letters
    channels = weight_ref.shape[1]
    vocab = table_ref.shape[0]
    tile = 256

    @pl.when(pl.program_id(0) == 0)
    def _():
        grad_ref[...] = jnp.zeros_like(grad_ref)
        table_ref[...] = jnp.zeros_like(table_ref)

    fewer = letters - narrow + 1

    @pl.when(pl.program_id(0) == 0)
    def _():
        share_ref[fewer * words:, tile:] = jnp.zeros((rows - fewer * words, channels - tile), jnp.bfloat16)

    def one_tile(c, count):
        scores_ref[: count * words] = jnp.dot(
            window_ref[: count * words], weight_ref[:, pl.ds(c, tile)], preferred_element_type=jnp.float32
        )
        for r in range(0, words, 16):
            top = pooled_ref[r:r + 16, pl.ds(c, tile)]
            part = share_in_ref[r:r + 16, pl.ds(c, tile)]
            for p in range(count):
                hit = scores_ref[p * words + r:p * words + r + 16] == top
                share_ref[p * words + r:p * words + r + 16, pl.ds(c, tile)] = jnp.where(hit, part, 0.0).astype(jnp.bfloat16)

    def later_tile(index, _):
        one_tile(pl.multiple_of(index * tile, tile), fewer)
        return 0

    one_tile(0, letters)
    lax.fori_loop(1, channels // tile, later_tile, 0)
    grad_ref[...] += jnp.dot(flipped_ref[...], share_ref[...], preferred_element_type=jnp.float32)
    scores_ref[:, :LANES] = jnp.dot(share_ref[...], turned_ref[...], preferred_element_type=jnp.float32)
    slot = lax.broadcasted_iota(jnp.int32, (words, LANES), 1) // 16
    for c in range(letters):
        spread = jnp.zeros((words, LANES), jnp.float32)
        for j in range(WIDTHS):
            if c - j >= 0:
                spread = jnp.where(slot == j, scores_ref[(c - j) * words:(c - j + 1) * words, :LANES], spread)
        spread_ref[c * words:(c + 1) * words] = spread.astype(jnp.bfloat16)
    onehot = jnp.where(lax.broadcasted_iota(jnp.int32, (vocab, rows), 0) == codes_ref[0], 1.0, 0.0).astype(jnp.bfloat16)
    table_ref[...] += jnp.dot(onehot, spread_ref[...], preferred_element_type=jnp.float32)


def conv_forward(spread, lens, weight, block):
    letters, words, _ = spread.shape
    channels = weight.shape[1]
    steps = words // block
    rows = letters * block
    f32 = jnp.float32
    return pl.pallas_call(
        conv_forward_kernel,
        grid=(steps,),
        in_specs=[
            pl.BlockSpec((letters, block, LANES), lambda i: (0, i, 0)),
            pl.BlockSpec((block, 1), lambda i: (i, 0)),
            pl.BlockSpec((LANES, channels), lambda i: (0, 0)),
        ],
        out_specs=[
            pl.BlockSpec((block, channels), lambda i: (i, 0)),
            pl.BlockSpec((block, channels), lambda i: (i, 0)),
            pl.BlockSpec((rows, LANES), lambda i: (i, 0)),
            pl.BlockSpec((LANES, rows), lambda i: (0, i)),
        ],
        out_shape=[
            jax.ShapeDtypeStruct((words, channels), f32),
            jax.ShapeDtypeStruct((words, channels), f32),
            jax.ShapeDtypeStruct((steps * rows, LANES), jnp.bfloat16),
            jax.ShapeDtypeStruct((LANES, steps * rows), jnp.bfloat16),
        ],
        scratch_shapes=[pltpu.VMEM((rows, 256), f32)],
        compiler_params=pltpu.CompilerParams(dimension_semantics=("arbitrary",)),
        cost_estimate=pl.CostEstimate(
            flops=2 * LANES * steps * rows * channels,
            bytes_accessed=steps * rows * channels * 5,
            transcendentals=0,
        ),
        name="conv_forward",
    )(spread, lens, weight)


def conv_backward(window, flipped, codes, weight, turned, pooled, share, vocab, block, first, steps, narrow):
    words, channels = pooled.shape
    rows = window.shape[0] // (words // block)
    letters = rows // block
    f32 = jnp.float32
    vocab = -(-vocab // 16) * 16

    def kernel(*refs):
        conv_backward_kernel(*refs, letters=letters, narrow=narrow)

    return pl.pallas_call(
        kernel,
        grid=(steps,),
        in_specs=[
            pl.BlockSpec((rows, LANES), lambda i: (first + i, 0)),
            pl.BlockSpec((LANES, rows), lambda i: (0, first + i)),
            pl.BlockSpec((1, 1, rows), lambda i: (first + i, 0, 0)),
            pl.BlockSpec((LANES, channels), lambda i: (0, 0)),
            pl.BlockSpec((channels, LANES), lambda i: (0, 0)),
            pl.BlockSpec((block, channels), lambda i: (first + i, 0)),
            pl.BlockSpec((block, channels), lambda i: (first + i, 0)),
        ],
        out_specs=[
            pl.BlockSpec((LANES, channels), lambda i: (0, 0)),
            pl.BlockSpec((vocab, LANES), lambda i: (0, 0)),
        ],
        out_shape=[
            jax.ShapeDtypeStruct((LANES, channels), f32),
            jax.ShapeDtypeStruct((vocab, LANES), f32),
        ],
        scratch_shapes=[
            pltpu.VMEM((rows, channels), jnp.bfloat16),
            pltpu.VMEM((rows, 256), f32),
            pltpu.VMEM((rows, LANES), jnp.bfloat16),
        ],
        compiler_params=pltpu.CompilerParams(dimension_semantics=("arbitrary",)),
        cost_estimate=pl.CostEstimate(
            flops=6 * LANES * steps * rows * channels,
            bytes_accessed=steps * rows * channels * 8,
            transcendentals=0,
        ),
        name="conv_backward",
    )(window, flipped, codes, weight, turned, pooled, share)


def merge_kernel(*refs):
    whole_ref = refs[-1]
    whole_ref[...] = jnp.zeros_like(whole_ref)
    features = refs[0].shape[0]
    first = 0
    for width, kernel_ref in enumerate(refs[:-1], 1):
        channels = kernel_ref.shape[1]
        whole_ref[: width * features, first : first + channels] = kernel_ref[...]
        marks = lax.broadcasted_iota(jnp.int32, (16, channels), 0) == width - 1
        whole_ref[WIDTHS * features :, first : first + channels] = jnp.where(marks, NEG, 0.0).astype(jnp.bfloat16)
        first = first + channels


def merged_weight(kernels):
    channels = sum(kernel.shape[1] for kernel in kernels)
    return pl.pallas_call(
        merge_kernel, out_shape=jax.ShapeDtypeStruct((LANES, channels), jnp.bfloat16), name="merge_widths"
    )(*kernels)


def spread_letters(codes, table):
    vocab, features = table.shape
    words, letters = codes.shape
    wide = jnp.tile(table, (1, LANES // features))
    onehot = (codes.T.reshape(-1, 1) == jnp.arange(vocab, dtype=jnp.int32)[None, :]).astype(jnp.bfloat16)
    return jnp.dot(onehot, wide, preferred_element_type=jnp.float32).astype(jnp.bfloat16).reshape(letters, words, LANES)


def score_heads(query_heads, key_heads, keep):
    raw = (
        jnp.einsum("qhd,khd->hqk", query_heads, key_heads, preferred_element_type=jnp.float32)
        * 0.125
    )
    return jnp.where(keep[None, None, :], raw, -1e30)


def body(
    character_codes,
    word_lengths,
    sequence_lengths,
    character_table,
    conv_width1,
    conv_width2,
    conv_width3,
    conv_width4,
    conv_width5,
    conv_width6,
    conv_width7,
    conv_bias,
    highway_weight,
    highway_bias,
    projection,
    position_table,
    attention_in,
    attention_out,
    norm1_gain,
    norm1_bias,
    hidden_in,
    hidden_out,
    norm2_gain,
    norm2_bias,
    cotangent,
):
    kernels = (
        conv_width1,
        conv_width2,
        conv_width3,
        conv_width4,
        conv_width5,
        conv_width6,
        conv_width7,
    )
    f32 = jnp.float32
    low = jnp.bfloat16
    side = lax.axis_index("seq")
    outer, middle, core = place()
    size = lax.axis_size("dp")
    chips = size // 2
    words = character_codes.shape[1]
    letters = character_codes.shape[2]
    vocab, features = character_table.shape
    filters = conv_bias.shape[0]
    mine = filters // 2
    piece = filters // size
    half = piece // 2
    model = position_table.shape[1]
    block = math.gcd(words, 64)
    steps = words // block

    highway_shard = own_blocks(highway_weight.reshape(-1, 2, filters), 2)
    held = lax.dynamic_slice_in_dim(projection, core * half, half, 0)
    lent = lax.dynamic_slice_in_dim(projection, (1 - core) * half, half, 0)
    projection_shard = jnp.where(core == side, held, core_swap(lent))
    code_rows = jnp.concatenate([character_codes[0], word_lengths[0][:, None]], axis=1)
    code_rows = [code_rows, seq_swap(code_rows)]

    highway_all = lax.all_gather(highway_shard.reshape(piece, filters), "dp", axis=0, tiled=True)
    highway_parts = [highway_all[:, :mine], highway_all[:, mine:]]
    projection_near = gather_near(outer_pieces(projection_shard))
    projection_across = middle_swap(projection_near)
    projection_far = [core_swap(projection_near), core_swap(projection_across)]
    projection_full = gather((projection_near, projection_across, *projection_far)).reshape(mine, model)
    attention_near = gather_near(
        outer_pieces(after(jnp.concatenate([attention_in, attention_out], axis=1), projection_near))
    )
    def cut(grad, slots=False):
        lead = (2, size // 4, 2) if slots else (size // 4, 2, 2)
        return grad.reshape(lead + (grad.shape[0] // size,) + grad.shape[1:])

    code_rows[1] = after(code_rows[1], projection_near)
    codes = [rows[:, :letters] for rows in code_rows]
    conv_weight = own_blocks(merged_weight(kernels), 1)
    conv_shift = own_blocks(conv_bias, 0).astype(f32)
    forwards = [
        conv_forward(spread_letters(codes[0], character_table), code_rows[0][:, letters:], conv_weight, block)
    ]
    rows = hidden_in.shape[0]
    splits = hidden_out.shape[0] // rows
    inner_size = hidden_in.shape[1]
    turned_in = hidden_in.reshape(rows, size, splits, rows).transpose(0, 2, 1, 3).reshape(rows, inner_size)
    forward_shard = jnp.concatenate(
        [turned_in] + [hidden_out[part * rows : (part + 1) * rows] for part in range(splits)], axis=1
    )
    forward_all = lax.all_gather(after(forward_shard, forwards[0][0]), "dp", axis=0, tiled=True)
    inward_full = forward_all[:, :inner_size]
    outward_parts = [
        forward_all[:, inner_size + part * model : inner_size + (part + 1) * model] for part in range(splits)
    ]
    forwards.append(
        conv_forward(spread_letters(codes[1], character_table), code_rows[1][:, letters:], conv_weight, block)
    )
    biased = [forward[0] + conv_shift for forward in forwards]
    hidden0_parts = [jax.nn.relu(value) for value in biased]
    hidden0_low = [value.astype(low) for value in hidden0_parts]
    swapped = [seq_swap(value) for value in hidden0_low]
    hidden0_all = jnp.concatenate(
        [interleave(hidden0_low[0], swapped[1], piece), interleave(hidden0_low[1], swapped[0], piece)], axis=0
    )
    hidden0 = jnp.concatenate(hidden0_parts, axis=0)
    highway_shift = own_blocks(highway_bias.reshape(2, filters), 1).astype(f32)
    transform, gate = [
        jnp.dot(hidden0_all, highway_parts[part], preferred_element_type=f32) + highway_shift[part]
        for part in range(2)
    ]
    hidden1 = highway_mix(transform, gate, hidden0)
    hidden1_low = hidden1.astype(low)
    attention_across = after(middle_swap(attention_near), hidden1_low)
    attention_far = [core_swap(attention_near), core_swap(attention_across)]
    attention_all = gather((attention_near, attention_across, *attention_far)).reshape(model, -1)
    attention_full = attention_all[:, : 3 * model]
    output_full = attention_all[:, 3 * model :]
    mapped = jnp.dot(hidden1_low, projection_full, preferred_element_type=f32)
    offset = side * words
    positions = lax.dynamic_slice_in_dim(position_table, offset, words, 0).astype(f32)
    embedded = mapped[:words] + seq_swap(mapped[words:].astype(low)).astype(f32) + positions
    embedded_low = embedded.astype(low)
    heads = model // HEAD_DIM
    projected = jnp.dot(embedded_low, attention_full, preferred_element_type=f32).astype(low)
    gathered = jnp.concatenate(
        [
            jnp.concatenate([pair, seq_swap(pair)], axis=0)
            for pair in (projected[:, model : 2 * model], projected[:, 2 * model :])
        ],
        axis=1,
    )
    length = gathered.shape[0]
    query_heads = projected[:, :model].reshape(words, heads, HEAD_DIM)
    key_heads = gathered[:, :model].reshape(length, heads, HEAD_DIM)
    value_heads = gathered[:, model:].reshape(length, heads, HEAD_DIM)
    keep = (jnp.arange(length, dtype=jnp.int32) + offset) % length < sequence_lengths[0]
    scores = score_heads(query_heads, key_heads, keep)
    top = jnp.max(scores, axis=-1, keepdims=True)
    unnormalized = jnp.exp(scores - top)
    total = jnp.sum(unnormalized, axis=-1, keepdims=True)
    probs_low = (unnormalized / total).astype(jnp.bfloat16)
    attended = jnp.einsum(
        "hqk,khd->qhd", probs_low, value_heads, preferred_element_type=jnp.float32
    )
    attended = attended.reshape(words, model).astype(jnp.bfloat16)
    joined = embedded + jnp.dot(attended, output_full, preferred_element_type=jnp.float32)
    gain1 = norm1_gain.astype(jnp.float32)
    shift1 = norm1_bias.astype(jnp.float32)
    gain2 = norm2_gain.astype(jnp.float32)
    shift2 = norm2_bias.astype(jnp.float32)
    normed1 = layer_norm(joined, gain1, shift1)
    normed1_low = normed1.astype(jnp.bfloat16)
    inner = jnp.dot(normed1_low, inward_full, preferred_element_type=jnp.float32)
    active = exact_gelu(inner).astype(jnp.bfloat16)
    actives = [active[:, part * model : (part + 1) * model] for part in range(splits)]
    summed = normed1 + sum(
        jnp.dot(actives[part], outward_parts[part], preferred_element_type=f32) for part in range(splits)
    )
    layer_out = layer_norm(summed, gain2, shift2).astype(jnp.bfloat16)
    seed_grad = cotangent[0].astype(jnp.float32)
    _, norm2_pull = jax.vjp(layer_norm, summed, gain2, shift2)
    grad_summed, norm2_gain_grad, norm2_bias_grad = norm2_pull(seed_grad)
    grad_outer = grad_summed.astype(jnp.bfloat16)
    hidden_out_grads = [
        jnp.einsum("tf,td->fd", part, grad_outer, preferred_element_type=f32).astype(low) for part in actives
    ]
    grad_active = jnp.concatenate(
        [jnp.einsum("td,fd->tf", grad_outer, part, preferred_element_type=f32) for part in outward_parts], axis=1
    )
    _, gelu_pull = jax.vjp(exact_gelu, inner)
    grad_inner = gelu_pull(grad_active)[0].astype(jnp.bfloat16)
    hidden_in_grad = jnp.einsum(
        "td,tf->df", normed1_low, grad_inner, preferred_element_type=jnp.float32
    ).astype(low)
    grad_normed1 = grad_summed + jnp.einsum(
        "tf,df->td", grad_inner, inward_full, preferred_element_type=jnp.float32
    )
    _, norm1_pull = jax.vjp(layer_norm, joined, gain1, shift1)
    grad_joined, norm1_gain_grad, norm1_bias_grad = norm1_pull(grad_normed1)
    forward_grad = jnp.concatenate([hidden_in_grad] + hidden_out_grads, axis=1)
    forward_sum = lax.psum_scatter(forward_grad, "dp", scatter_dimension=0, tiled=True)
    grad_branch = after(grad_joined.astype(low), forward_grad)
    attention_out_grad = jnp.einsum(
        "td,te->de", attended, grad_branch, preferred_element_type=jnp.float32
    ).astype(low)
    grad_attended = jnp.einsum(
        "te,de->td", grad_branch, output_full, preferred_element_type=jnp.float32
    ).astype(jnp.bfloat16)
    grad_heads = grad_attended.reshape(words, heads, HEAD_DIM)
    probs = jnp.exp(score_heads(query_heads, key_heads, keep) - top) / total
    probs_again = probs.astype(jnp.bfloat16)
    value_grad = jnp.einsum("hqk,qhd->khd", probs_again, grad_heads, preferred_element_type=f32)
    grad_probs = jnp.einsum(
        "qhd,khd->hqk", grad_heads, value_heads, preferred_element_type=jnp.float32
    )
    grad_scores = (
        probs * (grad_probs - jnp.sum(probs * grad_probs, axis=-1, keepdims=True))
    ).astype(jnp.bfloat16)
    grad_query = (
        jnp.einsum("hqk,khd->qhd", grad_scores, key_heads, preferred_element_type=jnp.float32)
        * 0.125
    )
    key_grad = (
        jnp.einsum("hqk,qhd->khd", grad_scores, query_heads, preferred_element_type=f32) * 0.125
    )
    value_grad = value_grad.reshape(length, model)
    key_grad = key_grad.reshape(length, model)
    value_back = seq_swap(value_grad[words:].astype(low))
    key_back = seq_swap(key_grad[words:].astype(low))
    grad_pairs = jnp.concatenate(
        [key_grad[:words] + key_back.astype(f32), value_grad[:words] + value_back.astype(f32)], axis=1
    )
    grad_projected = jnp.concatenate([grad_query.reshape(words, model), grad_pairs], axis=1).astype(low)
    attention_in_grad = jnp.einsum(
        "td,te->de", embedded_low, grad_projected, preferred_element_type=f32
    ).astype(low)
    grad_embedded = grad_joined + jnp.einsum(
        "te,de->td", grad_projected, attention_full, preferred_element_type=f32
    )
    grad_mapped = grad_embedded.astype(low)
    attention_half = scatter_core(cut(jnp.concatenate([attention_in_grad, attention_out_grad], axis=1)))
    grad_mapped = jnp.concatenate([grad_mapped, seq_swap(grad_mapped)], axis=0)
    grad_mapped = after(grad_mapped, attention_half)
    projection_grad = jnp.einsum(
        "tf,td->fd", hidden1_low, grad_mapped, preferred_element_type=f32
    ).astype(low)
    grad_hidden1 = jnp.einsum("td,fd->tf", grad_mapped, projection_full, preferred_element_type=f32)
    _, highway_pull = jax.vjp(highway_mix, transform, gate, hidden0)
    grad_transform, grad_gate, grad_carry = highway_pull(grad_hidden1)
    grad_gates = [grad_transform.astype(low), grad_gate.astype(low)]
    grad_spread = sum(
        jnp.einsum("tg,fg->tf", grad_gates[part], highway_parts[part], preferred_element_type=f32)
        for part in range(2)
    )
    grad_held, grad_lent = halves_of(grad_spread, piece)
    grad_lent = grad_lent.astype(low)
    lent_back = [seq_swap(grad_lent[words:]), seq_swap(grad_lent[:words])]
    highway_grads = [
        jnp.einsum("tf,tg->fg", hidden0_all, grad_gates[part], preferred_element_type=f32).astype(low)
        for part in range(2)
    ]
    joint_half = scatter_core(
        cut(jnp.concatenate([highway_grads[1], projection_grad.reshape(filters, model // 2)], axis=1))
    )
    attention_quarter = scatter_middle(attention_half)
    lent_back[1] = after(lent_back[1], joint_half, attention_quarter)
    grad_near = grad_carry + grad_held
    grad_pooled = [
        jnp.where(
            biased[part] > 0, grad_near[part * words : (part + 1) * words] + lent_back[part].astype(f32), 0.0
        )
        for part in range(2)
    ]
    highway_bias_grad = jnp.concatenate([jnp.sum(grad.astype(f32), axis=0) for grad in grad_gates])
    conv_bias_grad = jnp.sum(grad_pooled[0], axis=0) + jnp.sum(grad_pooled[1], axis=0)
    position_rows = 2 * words * model // mine // size
    position_low = grad_embedded.astype(low)
    nothing = jnp.zeros_like(position_low)
    position_grad = by_seq(position_low, nothing).reshape(size, position_rows, mine)
    highway_rows = jnp.concatenate(
        [highway_grads[0].reshape(size, piece, mine), position_grad], axis=1
    ).reshape(-1, mine)
    highway_sum = lax.psum_scatter(
        after(highway_rows, forward_sum), "dp", scatter_dimension=0, tiled=True
    )
    turned = conv_weight.T
    shares = [grad_pooled[part] / forwards[part][1] for part in range(2)]
    code_blocks = [
        codes[part].reshape(steps, block, letters).transpose(0, 2, 1).reshape(steps, 1, letters * block)
        for part in range(2)
    ]

    def back(part, first, count, *others):
        return conv_backward(
            forwards[part][2],
            forwards[part][3],
            code_blocks[part],
            conv_weight,
            turned,
            forwards[part][0],
            after(shares[part], *others),
            vocab,
            block,
            first,
            count,
            narrow,
        )

    cuts = steps // 2
    edges = [0]
    for kernel in kernels:
        edges.append(edges[-1] + kernel.shape[1])
    narrow = min(width for width in range(1, WIDTHS + 1) if edges[width] > 512)
    backs = [back(0, 0, cuts, attention_quarter, joint_half, highway_rows)]
    attention_sum = scatter_outer(attention_quarter, grad_pooled, backs[0])
    joint_quarter = scatter_middle(joint_half, (), backs[0])
    backs.append(back(0, cuts, steps - cuts, attention_sum, joint_quarter, *backs[0]))
    forward_both = forward_sum.astype(f32) + after(seq_swap(after(forward_sum, *backs[0])), *backs[1]).astype(f32)
    backs.append(back(1, 0, cuts, forward_sum, *backs[1]))
    attention_both = attention_sum + after(seq_swap(after(attention_sum.astype(low), *backs[1])), *backs[2]).astype(f32)
    backs.append(back(1, cuts, steps - cuts, forward_both, *backs[2]))
    joint_sum = scatter_outer(joint_quarter, backs[0], backs[3])
    merged_grad = backs[0][0] + backs[1][0] + backs[2][0] + backs[3][0]
    table_wide = backs[0][1] + backs[1][1] + backs[2][1] + backs[3][1]
    table_grad = sum(
        table_wide[:vocab, shift * features : (shift + 1) * features] for shift in range(WIDTHS)
    )

    forward_total = forward_both
    inward_total = (
        forward_total[:, :inner_size].reshape(rows, splits, size, rows).transpose(0, 2, 1, 3).reshape(rows, inner_size)
    )
    outward_total = jnp.concatenate(
        [forward_total[:, inner_size + part * model : inner_size + (part + 1) * model] for part in range(splits)],
        axis=0,
    )
    attention_total = attention_both[:, : 3 * model]
    output_total = attention_both[:, 3 * model :]
    part0 = highway_sum[:piece]
    position_part = highway_sum[piece:]
    position_part = (position_part.astype(f32) + seq_swap(position_part).astype(f32)).astype(low)
    part1 = joint_sum.astype(low)
    projection_part = part1[:, mine:].reshape(half, model)
    projection_pair = core_swap(projection_part)
    projection_sum = jnp.concatenate(
        [
            jnp.where(core == 0, projection_part, projection_pair),
            jnp.where(core == 0, projection_pair, projection_part),
        ],
        axis=0,
    )
    finals = jnp.concatenate([part0, part1[:, :mine], projection_sum], axis=1)
    finals_other = seq_swap(finals)
    projection_total = jnp.where(core == side, finals[:, 2 * mine :], finals_other[:, 2 * mine :]).astype(f32)
    highway_total = (
        by_seq(
            finals[:, : 2 * mine].reshape(piece, 2, chips, piece),
            finals_other[:, : 2 * mine].reshape(piece, 2, chips, piece),
        )
        .transpose(1, 2, 3, 0, 4)
        .reshape(piece, 2 * filters)
        .astype(f32)
    )

    conv_rows = WIDTHS * features
    table_rows = -(-vocab * features // mine)
    table_flat = jnp.pad(table_grad.reshape(-1), (0, table_rows * mine - vocab * features))
    entries = [
        merged_grad[:conv_rows],
        conv_bias_grad[None],
        highway_bias_grad.reshape(2, mine),
        table_flat.reshape(table_rows, mine),
        jnp.concatenate([norm1_gain_grad, norm1_bias_grad, norm2_gain_grad, norm2_bias_grad]).reshape(-1, mine),
    ]
    starts = [0]
    for row in entries:
        starts.append(starts[-1] + row.shape[0])
    padded = -(-starts[-1] // size) * size
    small = jnp.pad(jnp.concatenate(entries, axis=0), ((0, padded - starts[-1]), (0, 0)))
    small = after(small, joint_sum, attention_both, highway_sum)
    small = scatter_outer(scatter_middle(scatter_core(cut(small)))).astype(low)
    share = small.shape[0]
    small = after(jnp.concatenate([small, seq_swap(small), position_part], axis=0), finals_other)
    near = gather_near(outer_pieces(small))
    across = middle_swap(near)
    small = gather((near, across, core_swap(near), core_swap(across))).reshape(size, -1, mine)
    small_own = small[:, :share].reshape(padded, mine)
    small_other = small[:, share : 2 * share].reshape(padded, mine)
    own = [small_own[starts[i] : starts[i + 1]] for i in range(len(entries))]
    other = [small_other[starts[i] : starts[i + 1]] for i in range(len(entries))]
    conv_all = (
        by_seq(own[0].reshape(conv_rows, chips, piece), other[0].reshape(conv_rows, chips, piece))
        .transpose(1, 2, 0, 3)
        .reshape(conv_rows, filters)
        .astype(f32)
    )
    conv_bias_total = (
        by_seq(own[1].reshape(chips, piece), other[1].reshape(chips, piece))
        .transpose(1, 0, 2)
        .reshape(filters)
        .astype(f32)
    )
    highway_bias_total = (
        by_seq(own[2].reshape(2, chips, piece), other[2].reshape(2, chips, piece))
        .transpose(1, 2, 0, 3)
        .reshape(2 * filters)
        .astype(f32)
    )
    table_total = (own[3].astype(f32) + other[3].astype(f32)).reshape(-1)
    table_total = table_total[: vocab * features].reshape(vocab, features)
    norms = (own[4].astype(f32) + other[4].astype(f32)).reshape(4, model)
    position_total = small[:, 2 * share :].reshape(2 * words, model).astype(f32)
    kernel_grads = []
    first = 0
    for kernel in kernels:
        kernel_grads.append(conv_all[: kernel.shape[0], first : first + kernel.shape[1]])
        first = first + kernel.shape[1]
    return (
        layer_out[None],
        table_total,
        *kernel_grads,
        conv_bias_total,
        highway_total,
        highway_bias_total,
        projection_total,
        position_total,
        attention_total,
        output_total,
        norms[0],
        norms[1],
        inward_total,
        outward_total,
        norms[2],
        norms[3],
    )


def solution(mesh):
    placed = (
        P("dp", "seq", None),
        P("dp", "seq"),
        P("dp"),
        P(),
        P(),
        P(),
        P(),
        P(),
        P(),
        P(),
        P(),
        P(),
        P("dp", None),
        P(),
        P("dp", None),
        P(),
        P("dp", None),
        P("dp", None),
        P(),
        P(),
        P("dp", None),
        P("dp", None),
        P(),
        P(),
        P("dp", "seq", None),
    )
    return jax.shard_map(
        body,
        mesh=mesh,
        in_specs=placed,
        out_specs=(
            P("dp", "seq", None),
            P(),
            P(),
            P(),
            P(),
            P(),
            P(),
            P(),
            P(),
            P(),
            P("dp", None),
            P(),
            P("dp", None),
            P(),
            P("dp", None),
            P("dp", None),
            P(),
            P(),
            P("dp", None),
            P("dp", None),
            P(),
            P(),
        ),
        check_vma=False,
    )
```
